128 devices in a mesh: gx: 16 (over x, z_lo, core), gy: 8 (over y, z_hi).
Axes of the slice: x: 4, y: 4, z: 4 (z_hi: 2, z_lo: 2; z = z_hi * 2 + z_lo), core: 2. Of those that a mesh axis runs over, the one named last changes fastest.
Arguments:
- observed: float32 [256, 256, 768], P('gx', 'gy'), may hold values from -60 to 60, as said below
- psf_taps: float32 [3, 31], replicated, may hold values from 0.02 to 0.1
Outputs:
- solution: float32 [256, 256, 768], P('gx', 'gy')
The draws below stay inside these ranges and needn't reach their ends.
Inputs may be any that keep to these rules, and one draw needn't show every extreme that they name: `observed`: entries are finite reals of order one to some tens.
All inputs are finite; a program needn't handle non-finite values.
Results may differ from the reference program's by a relative error of at most 0.0003.
Values sent between devices are 32-bit elements; how exact they have to be, the bound alone decides.
No kernel may reach another device: no remote copies, remote signals or barrier semaphores. Data moves between devices by JAX's collectives and lax.ppermute only.
A program may use at most 64 MiB of HBM per device.

```python
import jax
import jax.numpy as jnp
from jax import lax

NZ = 768
TAPS = 31
NX = 256
NY = 256


def draw_observed(key, part):
    key_noise = jax.random.fold_in(jax.random.fold_in(key, 7), 0)
    x_frac = jnp.arange(NX).astype(jnp.float32) / max(NX - 1, 1)
    y_frac = jnp.arange(NY).astype(jnp.float32) / max(NY - 1, 1)
    rising = jnp.sqrt((1.0 + 2.0 * x_frac)[:, None, None] * (1.0 + 2.0 * y_frac)[None, :, None])
    values = jax.random.normal(key_noise, (NX, NY, NZ), jnp.float32) * rising
    return jnp.clip(values, -60.0, 60.0)


def setup_inputs(seed: int = 0) -> dict:
    streams_of = jax.random.split(jax.random.key(seed), 3)
    return {
        "observed": draw_observed(jax.random.fold_in(streams_of[2], 71), 0),
        "psf_taps": jnp.clip(jax.random.uniform(streams_of[1], (3, TAPS), jnp.float32, 0.02, 0.1), 0.02, 0.1),
    }


def filter_dim(padded, kernel, which_dim, length):
    summed = kernel[0] * lax.slice_in_dim(padded, 30, 30 + length, axis=which_dim)
    for offset in range(1, 31):
        summed = summed + kernel[offset] * lax.slice_in_dim(padded, 30 - offset, 30 - offset + length, axis=which_dim)
    return summed

def wrap_rims(field, which_dim):
    length = field.shape[which_dim]
    lower = lax.slice_in_dim(field, length - 15, length, axis=which_dim)
    upper = lax.slice_in_dim(field, 0, 15, axis=which_dim)
    return jnp.concatenate([lower, field, upper], axis=which_dim)

def convolve(field, kernel):
    for which_dim in range(3):
        field = filter_dim(wrap_rims(field, which_dim), kernel[which_dim], which_dim, field.shape[which_dim])
    return field

def tikhonov(alpha_one, beta_two, alpha_two, beta_three, beta_one):
    gram_aa = alpha_one * alpha_one + beta_two * beta_two
    gram_ab = beta_two * alpha_two
    gram_bb = alpha_two * alpha_two + beta_three * beta_three
    target = alpha_one * beta_one
    grid_exp = jnp.arange(16).astype(jnp.float32) * (3.0 / 15.0) - 3.0
    lambdas = alpha_one * jnp.power(10.0, grid_exp)

    def project(squared):
        entry_a = gram_aa + squared
        entry_b = gram_bb + squared
        determ = entry_a * entry_b - gram_ab * gram_ab
        return (entry_b * target / determ, -gram_ab * target / determ, entry_a, entry_b, determ)
    coef_one, coef_two, entry_a, entry_b, determ = project(lambdas * lambdas)
    miss_one = beta_one - alpha_one * coef_one
    miss_two = -(beta_two * coef_one + alpha_two * coef_two)
    miss_three = -beta_three * coef_two
    trace_sum = (entry_b * gram_aa - 2.0 * gram_ab * gram_ab + entry_a * gram_bb) / determ
    scores = 3.0 * (miss_one * miss_one + miss_two * miss_two + miss_three * miss_three) / ((3.0 - trace_sum) ** 2 * beta_one * beta_one)
    weights = 1.0 / (scores + 0.05) ** 4
    chosen = jnp.exp(jnp.sum(weights * jnp.log(lambdas)) / jnp.sum(weights))
    coef_one, coef_two, entry_a, entry_b, determ = project(chosen * chosen)
    return (coef_one, coef_two)

def reference(observed, psf_taps):
    flipped = psf_taps[:, ::-1]
    beta_one = jnp.sqrt(jnp.sum(observed * observed))
    left_one = observed / beta_one
    back = convolve(left_one, flipped)
    alpha_one = jnp.sqrt(jnp.sum(back * back))
    right_one = back / alpha_one
    forward = convolve(right_one, psf_taps) - alpha_one * left_one
    beta_two = jnp.sqrt(jnp.sum(forward * forward))
    left_two = forward / beta_two
    back = convolve(left_two, flipped) - beta_two * right_one
    alpha_two = jnp.sqrt(jnp.sum(back * back))
    right_two = back / alpha_two
    forward = convolve(right_two, psf_taps) - alpha_two * left_two
    beta_three = jnp.sqrt(jnp.sum(forward * forward))
    coef_one, coef_two = tikhonov(alpha_one, beta_two, alpha_two, beta_three, beta_one)
    return coef_one * right_one + coef_two * right_two
```

```python
import jax
import jax.numpy as jnp
import numpy as np
from jax import lax
from jax.experimental import pallas as pl
from jax.experimental.pallas import tpu as pltpu
from jax.sharding import PartitionSpec as P

NX, NY, NZ, TAPS = 256, 256, 768, 31
HALF = TAPS // 2
F32, BF16 = jnp.float32, jnp.bfloat16
TINY = 1e-30


def real_basis(n):
    pos = np.arange(n)
    basis = np.zeros((n, n))
    partner = np.zeros((n, n))
    basis[0] = 1.0 / np.sqrt(n)
    basis[1] = np.where(pos % 2 == 0, 1.0, -1.0) / np.sqrt(n)
    for f in range(1, n // 2):
        angle = 2.0 * np.pi * ((f * pos) % n) / n
        basis[2 * f] = np.sqrt(2.0 / n) * np.cos(angle)
        basis[2 * f + 1] = np.sqrt(2.0 / n) * np.sin(angle)
        partner[2 * f] = -basis[2 * f + 1]
        partner[2 * f + 1] = basis[2 * f]
    return basis, partner


def halves(values):
    hi = np.asarray(values, np.float32).astype(BF16)
    lo = (values - hi.astype(np.float64)).astype(np.float32).astype(BF16)
    return hi, lo


def split(values):
    hi = values.astype(BF16)
    return hi, (values - hi.astype(F32)).astype(BF16)


def dot3(left, right, dims=((1,), (0,))):
    def one(a, b):
        return lax.dot_general(a, b, (dims, ((), ())), preferred_element_type=F32)

    return one(left[0], right[0]) + (one(left[0], right[1]) + one(left[1], right[0]))


def total(values):
    return jnp.sum(values, axis=(0, 1), keepdims=True)


def response(freq, taps, n):
    offset = lax.broadcasted_iota(jnp.int32, freq.shape, 1).astype(F32) - float(HALF)
    turn = freq * offset
    turn = turn - float(n) * jnp.floor(turn * (1.0 / n))
    angle = turn * (2.0 * np.pi / n)
    return (
        jnp.sum(jnp.cos(angle) * taps, axis=1, keepdims=True),
        jnp.sum(jnp.sin(angle) * taps, axis=1, keepdims=True),
    )


def taps_kernel(dev_ref, taps_ref, qtx_ref, ptx_ref, qy_ref, py_ref, lam_ref, mxh_ref, mxl_ref, myh_ref, myl_ref, zed_ref):
    row = lax.broadcasted_iota(jnp.int32, (NX, TAPS), 0)
    freq = jnp.where(row == 1, NX // 2, row // 2).astype(F32)
    re_x, im_x = response(freq, taps_ref[0:1, :], NX)
    re_y, im_y = response(freq, taps_ref[1:2, :], NY)
    lane = lax.broadcasted_iota(jnp.int32, (NX, 128), 1)
    lam_y = re_y * re_y + im_y * im_y
    rows = jnp.where(lane == 0, re_x, jnp.where(lane == 1, im_x, lam_y)).T
    lam_ref[...] = (re_x * re_x + im_x * im_x) * rows[2:3, :]
    mxh_ref[...], mxl_ref[...] = split(qtx_ref[...] * rows[0:1, :] + ptx_ref[...] * rows[1:2, :])
    myh_ref[...], myl_ref[...] = split(qy_ref[...] * re_y + py_ref[...] * im_y)
    which = lax.broadcasted_iota(jnp.int32, (8, TAPS), 0)
    pair = dev_ref[0] * 3 + which // 2
    odd = which % 2
    first = pair == 0
    freq = jnp.where(first & (odd == 1), NZ // 2, pair).astype(F32)
    re_z, im_z = response(freq, taps_ref[2:3, :], NZ)
    im_z = jnp.where(first[:, 0:1], 0.0, im_z)
    zed_ref[0:8, :] = jnp.broadcast_to(re_z, (8, 256))
    zed_ref[8:16, :] = jnp.broadcast_to(jnp.where(odd[:, 0:1] == 1, -im_z, im_z), (8, 256))
    zed_ref[16:24, :] = jnp.broadcast_to(re_z * re_z + im_z * im_z, (8, 256))


def forward_z_kernel(cells_ref, fh_ref, fl_ref, out_ref):
    basis = (fh_ref[...], fl_ref[...])
    for n in range(2):
        cells = split(cells_ref[n * 256 : (n + 1) * 256, :])
        freqs = dot3(basis, cells, ((1,), (1,)))
        for k in range(6):
            for c in range(2):
                out_ref[pl.ds((2 * n + c) * 6 + k, 128, stride=24), :] = freqs[k * 128 : (k + 1) * 128, c * 128 : (c + 1) * 128]


def inverse_z_kernel(in_ref, fh_ref, fl_ref, out_ref):
    basis = (fh_ref[...], fl_ref[...])
    for c in range(4):
        freqs = jnp.concatenate([in_ref[pl.ds(c * 6 + k, 128, stride=24), :] for k in range(6)], axis=0)
        out_ref[c * 128 : (c + 1) * 128, :] = dot3(split(freqs.T), basis)


def swap_blocks(vecs, block):
    low = block < 2
    even = (block % 2) == 0

    def roll(x, by):
        return pltpu.roll(x, by, 1)

    v0, v1, v2, v3 = vecs
    u0, u2 = jnp.where(low, v0, roll(v2, 64)), jnp.where(low, roll(v0, 64), v2)
    u1, u3 = jnp.where(low, v1, roll(v3, 64)), jnp.where(low, roll(v1, 64), v3)
    w0, w1 = jnp.where(even, u0, roll(u1, 32)), jnp.where(even, roll(u0, 96), u1)
    w2, w3 = jnp.where(even, u2, roll(u3, 32)), jnp.where(even, roll(u2, 96), u3)
    return w0, w1, w2, w3


def forward_xy_kernel(in_ref, lam_ref, zed_ref, qxh_ref, qxl_ref, qth_ref, qtl_ref, spec_ref, stat_ref, lo_ref, hi_ref):
    block = lax.broadcasted_iota(jnp.int32, (24, 128), 1) // 32
    halves_ref = (lo_ref, hi_ref)

    def gather(i, carry):
        for high in range(2):
            got = [in_ref[pl.ds(pl.multiple_of((i * 8 + high * 4 + j) * 24, 8), 24), :] for j in range(4)]
            for r, piece in enumerate(swap_blocks(got, block)):
                halves_ref[high][pl.ds(pl.multiple_of((i * 4 + r) * 24, 8), 24), :] = piece
        return carry

    lax.fori_loop(0, 16, gather, 0)
    rows = jnp.concatenate([lo_ref[...], hi_ref[...]], axis=1)
    rows = dot3(split(rows), (qth_ref[...], qtl_ref[...]))
    lo_ref[...], hi_ref[...] = rows[:, :128], rows[:, 128:]
    left = (qxh_ref[...], qxl_ref[...])
    for k in range(6):
        plane = jnp.concatenate([ref[pl.ds(k, 256, stride=6), :] for ref in halves_ref], axis=1)
        spec_ref[k] = dot3(left, split(plane))

    def sums(*funcs):
        parts = [jnp.zeros((8, 256), F32) for _ in funcs]
        for k in range(6):
            spec = spec_ref[k]
            lam = lam_ref[...] * zed_ref[16 + k : 17 + k, :]
            power = spec * spec
            for n, func in enumerate(funcs):
                parts[n] = parts[n] + jnp.sum(func(power, lam).reshape(32, 8, 256), axis=0)
        return [total(p) for p in parts]

    zero, one, two = sums(lambda w, l: w, lambda w, l: w * l, lambda w, l: w * l * l)
    mean = one / jnp.maximum(zero, TINY)
    tau = two / jnp.maximum(one, TINY)

    def centred(w, l):
        d = l - mean
        return w * d * d

    def tilted(w, l):
        d = l - tau
        return w * l * d * d

    var, tilt = sums(centred, tilted)
    step = tau - mean
    slope = (tilt + one * step * step) / jnp.maximum(var, TINY)
    ratio = var / jnp.maximum(zero, TINY)

    def second(w, l):
        d = (l - slope) * (l - mean) - ratio
        return w * d * d

    (last,) = sums(second)
    lane = lax.broadcasted_iota(jnp.int32, (128, 128), 1)
    packed = jnp.zeros((128, 128), F32)
    for n, value in enumerate((zero, mean, tau, var, slope, ratio, tilt, last, one)):
        packed = jnp.where(lane == n, value, packed)
    stat_ref[...] = packed


def weights_of(stats):
    zero, mean, tau, var, slope, ratio, tilt, last, one = [stats[n : n + 1, :] for n in range(9)]

    def add(x):
        return jnp.sum(x, axis=1, keepdims=True)

    all_zero = add(zero)
    all_mean = add(one) / all_zero
    shift = mean - all_mean
    all_var = add(var + shift * shift * zero)
    all_ratio = all_var / all_zero
    lean = tau - all_mean
    all_slope = add(tilt + one * lean * lean) / all_var
    lean = tau - all_mean - all_var / (all_zero * all_mean)
    all_tilt = add(tilt + one * lean * lean)
    first = shift + (slope - all_slope)
    const = shift * (mean - all_slope) + ratio - all_ratio
    all_last = add(last + first * first * var + const * const * zero)

    beta_one = jnp.sqrt(all_zero)
    alpha_one = jnp.sqrt(all_mean)
    beta_two = jnp.sqrt(all_var / (all_zero * all_mean))
    alpha_two = jnp.sqrt(all_tilt / all_var)
    beta_three = jnp.sqrt(all_last / all_tilt)

    gram_aa = alpha_one * alpha_one + beta_two * beta_two
    gram_ab = beta_two * alpha_two
    gram_bb = alpha_two * alpha_two + beta_three * beta_three
    target = alpha_one * beta_one
    lane = lax.broadcasted_iota(jnp.int32, (1, 128), 1)
    log_grid = (jnp.minimum(lane, 15).astype(F32) * 0.2 - 3.0) * float(np.log(10.0))
    lambdas = alpha_one * jnp.exp(log_grid)

    def project(squared):
        entry_a = gram_aa + squared
        entry_b = gram_bb + squared
        determ = entry_a * entry_b - gram_ab * gram_ab
        return (entry_b * target / determ, -gram_ab * target / determ, entry_a, entry_b, determ)

    coef_one, coef_two, entry_a, entry_b, determ = project(lambdas * lambdas)
    miss_one = beta_one - alpha_one * coef_one
    miss_two = -(beta_two * coef_one + alpha_two * coef_two)
    miss_three = -beta_three * coef_two
    trace_sum = (entry_b * gram_aa - 2.0 * gram_ab * gram_ab + entry_a * gram_bb) / determ
    left = 3.0 - trace_sum
    scores = (
        3.0
        * (miss_one * miss_one + miss_two * miss_two + miss_three * miss_three)
        / (left * left * beta_one * beta_one)
    )
    shifted = scores + 0.05
    shifted = shifted * shifted
    weights = jnp.where(lane < 16, 1.0 / (shifted * shifted), 0.0)
    chosen = jnp.exp(add(weights * jnp.log(lambdas)) / add(weights))
    coef_one, coef_two, entry_a, entry_b, determ = project(chosen * chosen)
    scale = 1.0 / (alpha_one * beta_one)
    lead = coef_two / alpha_two
    c2 = lead * scale / beta_two
    c1 = coef_one * scale - lead * (alpha_one / (beta_one * beta_two) + beta_two * scale)
    return c1, c2


def inverse_xy_kernel(stat_ref, spec_ref, lam_ref, zed_ref, mxh_ref, mxl_ref, myh_ref, myl_ref, out_ref, lo_ref, hi_ref):
    halves_ref = (lo_ref, hi_ref)
    c1, c2 = weights_of(stat_ref[...].T)
    left = (mxh_ref[...], mxl_ref[...])
    for p in range(3):
        even, odd = 2 * p, 2 * p + 1
        lam = lam_ref[...]
        a = (c1 + c2 * (lam * zed_ref[16 + even : 17 + even, :])) * spec_ref[even]
        b = (c1 + c2 * (lam * zed_ref[16 + odd : 17 + odd, :])) * spec_ref[odd]
        turned_a = zed_ref[even : even + 1, :] * a + zed_ref[8 + even : 9 + even, :] * b
        turned_b = zed_ref[odd : odd + 1, :] * b + zed_ref[8 + odd : 9 + odd, :] * a
        for k, plane in ((even, turned_a), (odd, turned_b)):
            back = dot3(left, split(plane))
            for h in range(2):
                halves_ref[h][pl.ds(k, 256, stride=6), :] = back[:, h * 128 : (h + 1) * 128]
    rows = jnp.concatenate([lo_ref[...], hi_ref[...]], axis=1)
    rows = dot3(split(rows), (myh_ref[...], myl_ref[...]))
    lo_ref[...], hi_ref[...] = rows[:, :128], rows[:, 128:]
    block = lax.broadcasted_iota(jnp.int32, (24, 128), 1) // 32

    def scatter(i, carry):
        for high in range(2):
            got = [
                halves_ref[high][pl.ds(pl.multiple_of((i * 4 + r) * 24, 8), 24), :] for r in range(4)
            ]
            for j, piece in enumerate(swap_blocks(got, block)):
                out_ref[pl.ds(pl.multiple_of((i * 8 + high * 4 + j) * 24, 8), 24), :] = piece
        return carry

    lax.fori_loop(0, 16, scatter, 0)


def sds(shape, dtype=F32):
    return jax.ShapeDtypeStruct(shape, dtype)


def make_local():
    vmem = pl.BlockSpec(memory_space=pltpu.VMEM)
    smem = pl.BlockSpec(memory_space=pltpu.SMEM)
    params = pltpu.CompilerParams(vmem_limit_bytes=48 << 20)

    basis_z, _ = real_basis(NZ)
    order = (6 * np.arange(128)[None, :] + np.arange(6)[:, None]).reshape(-1)
    fz = halves(basis_z[order])
    basis, partner = real_basis(NX)
    place = np.arange(NX)
    i, r, c = place // 16, (place // 4) % 4, place % 4
    where = 16 * i + 4 * c + r
    qx = halves(basis[:, where])
    qtx = basis[:, where].T.astype(np.float32)
    ptx = partner[:, where].T.astype(np.float32)
    qt = halves(basis.T)
    qy = basis.astype(np.float32)
    py = partner.astype(np.float32)

    def local(observed, psf_taps):
        dev = (lax.axis_index("gx") * 8 + lax.axis_index("gy")).astype(jnp.int32).reshape(1)
        lam, mxh, mxl, myh, myl, zed = pl.pallas_call(
            taps_kernel,
            in_specs=[smem] + [vmem] * 5,
            out_specs=[vmem] * 6,
            out_shape=[sds((NX, NY))] + [sds((NX, NX), BF16)] * 4 + [sds((24, 256))],
            name="taps_kernel",
        )(dev, psf_taps, qtx, ptx, qy, py)
        sent = pl.pallas_call(
            forward_z_kernel,
            in_specs=[vmem] * 3,
            out_specs=vmem,
            out_shape=sds((3072, 128)),
            compiler_params=params,
            name="forward_z",
        )(observed.reshape(512, NZ), *fz)
        got = lax.all_to_all(sent.reshape(128, 24, 128), ("gx", "gy"), 0, 0, tiled=True).reshape(3072, 128)
        spec, stat = pl.pallas_call(
            forward_xy_kernel,
            in_specs=[vmem] * 7,
            out_specs=[vmem] * 2,
            out_shape=[sds((6, NX, NY)), sds((128, 128))],
            scratch_shapes=[pltpu.VMEM((1536, 128), F32)] * 2,
            compiler_params=params,
            name="forward_xy",
        )(got, lam, zed, *qx, *qt)
        stats = lax.all_to_all(stat.reshape(128, 1, 128), ("gx", "gy"), 0, 0, tiled=True).reshape(128, 128)
        sent = pl.pallas_call(
            inverse_xy_kernel,
            in_specs=[vmem] * 8,
            out_specs=vmem,
            out_shape=sds((3072, 128)),
            scratch_shapes=[pltpu.VMEM((1536, 128), F32)] * 2,
            compiler_params=params,
            name="inverse_xy",
        )(stats, spec, lam, zed, mxh, mxl, myh, myl)
        got = lax.all_to_all(sent.reshape(128, 24, 128), ("gx", "gy"), 0, 0, tiled=True).reshape(3072, 128)
        out = pl.pallas_call(
            inverse_z_kernel,
            in_specs=[vmem] * 3,
            out_specs=vmem,
            out_shape=sds((512, NZ)),
            compiler_params=params,
            name="inverse_z",
        )(got, *fz)
        return out.reshape(16, 32, NZ)

    return local


def solution(mesh):
    in_specs = (P("gx", "gy", None), P())
    out_specs = P("gx", "gy", None)
    return jax.shard_map(make_local(), mesh=mesh, in_specs=in_specs, out_specs=out_specs, check_vma=False)
```

```python
import jax
import jax.numpy as jnp
import numpy as np
from jax import lax
from jax.experimental import pallas as pl
from jax.experimental.pallas import tpu as pltpu
from jax.sharding import PartitionSpec as P

NX, NY, NZ, TAPS = 256, 256, 768, 31
HALF = TAPS // 2
THIRD = NZ // 3
ROOT3 = float(np.sqrt(3.0) / 2.0)
F32, BF16 = jnp.float32, jnp.bfloat16
TINY = 1e-30
NN = ((1,), (0,))
NT = ((1,), (1,))


def halves(values):
    hi = np.asarray(values, np.float32).astype(BF16)
    lo = (values - hi.astype(np.float64)).astype(np.float32).astype(BF16)
    return hi, lo


def plane_basis(n):
    pos = np.arange(n)
    freq = np.arange(n // 2)[:, None]
    angle = 2.0 * np.pi * ((freq * pos) % n) / n
    basis = np.concatenate([np.cos(angle), np.sin(angle)]) * np.sqrt(2.0 / n)
    basis[0] = 1.0 / np.sqrt(n)
    basis[n // 2] = np.where(pos % 2 == 0, 1.0, -1.0) / np.sqrt(n)
    return basis


def plane_table(n):
    freq = np.arange(n) % (n // 2)
    freq[n // 2] = n // 2
    offset = np.arange(TAPS) - HALF
    turn = (freq[:, None] * offset) % n
    sine = np.where(turn % (n // 2) == 0, 0.0, np.sin(2.0 * np.pi * turn / n))
    table = np.zeros((2 * n, 128))
    table[:n, :TAPS] = np.cos(2.0 * np.pi * turn / n)
    table[n:, :TAPS] = sine
    return table


def depth_basis():
    pos = np.arange(THIRD)
    dev = np.arange(128)[:, None]
    scale = np.sqrt(2.0 / NZ)

    def angle(freq):
        return 2.0 * np.pi * ((freq * pos) % NZ) / NZ

    cos0, sin0 = scale * np.cos(angle(3 * dev)), scale * np.sin(angle(3 * dev))
    cos0[0] = 1.0 / np.sqrt(NZ)
    sin0[0] = np.where(pos % 2 == 0, 1.0, -1.0) / np.sqrt(NZ)
    first = np.concatenate([cos0, sin0])
    rest = []
    for step, sign in ((1, 1.0), (2, -1.0)):
        cos, sin = scale * np.cos(angle(3 * dev + step)), scale * np.sin(angle(3 * dev + step))
        rest.append(np.concatenate([cos, -sign * sin], axis=1))
        rest.append(np.concatenate([sin, sign * cos], axis=1))
    return first, np.concatenate(rest)


def split(values):
    hi = values.astype(BF16)
    return hi, (values - hi.astype(F32)).astype(BF16)


def dot3(left, right, dims=NN):
    def one(a, b):
        return lax.dot_general(a, b, (dims, ((), ())), preferred_element_type=F32)

    return one(left[0], right[0]) + (one(left[0], right[1]) + one(left[1], right[0]))


def total(values):
    return jnp.sum(values, axis=(0, 1), keepdims=True)


def padded_taps(taps_ref, pad_ref):
    pad_ref[...] = jnp.zeros((8, 128), F32)
    pad_ref[0:3, 0:TAPS] = taps_ref[...]
    return pad_ref[...]


def depth_response(dev, taps):
    row = lax.broadcasted_iota(jnp.int32, (8, 128), 0)
    offset = lax.broadcasted_iota(jnp.int32, (8, 128), 1).astype(F32) - float(HALF)
    pair = dev * 3 + row // 2
    odd = row % 2
    first = pair == 0
    freq = jnp.where(first & (odd == 1), NZ // 2, pair).astype(F32)
    turn = freq * offset
    turn = turn - float(NZ) * jnp.floor(turn * (1.0 / NZ))
    angle = turn * (2.0 * np.pi / NZ)
    real = jnp.sum(jnp.cos(angle) * taps, axis=1, keepdims=True)
    imag = jnp.sum(jnp.where(first, 0.0, jnp.sin(angle)) * taps, axis=1, keepdims=True)
    return real, jnp.where(odd[:, 0:1] == 1, -imag, imag), real * real + imag * imag


def swap_blocks(vecs, block):
    low = block < 2
    even = (block % 2) == 0

    def roll(x, by):
        return pltpu.roll(x, by, 1)

    v0, v1, v2, v3 = vecs
    u0, u2 = jnp.where(low, v0, roll(v2, 64)), jnp.where(low, roll(v0, 64), v2)
    u1, u3 = jnp.where(low, v1, roll(v3, 64)), jnp.where(low, roll(v1, 64), v3)
    w0, w1 = jnp.where(even, u0, roll(u1, 32)), jnp.where(even, roll(u0, 96), u1)
    w2, w3 = jnp.where(even, u2, roll(u3, 32)), jnp.where(even, roll(u2, 96), u3)
    return w0, w1, w2, w3


def forward_z_kernel(cells_hbm, ah_hbm, al_hbm, bh_hbm, bl_hbm, out_ref, cells, ah, al, bh, bl, sems):
    copies = [pltpu.make_async_copy(cells_hbm.at[pl.ds(n * 256, 256)], cells.at[pl.ds(n * 256, 256)], sems.at[n]) for n in range(2)]
    pairs = ((ah_hbm, ah), (al_hbm, al), (bh_hbm, bh), (bl_hbm, bl))
    copies += [pltpu.make_async_copy(src, dst, sems.at[2 + n]) for n, (src, dst) in enumerate(pairs)]
    order = (0, 2, 3, 4, 5, 1)
    for n in order:
        copies[n].start()
    for n in range(2):
        copies[n].wait()
        b0, b1, b2 = [cells[n * 256 : (n + 1) * 256, m * THIRD : (m + 1) * THIRD] for m in range(3)]
        both = b1 + b2
        whole = split(b0 + both)
        rest = split(jnp.concatenate([b0 - 0.5 * both, ROOT3 * (b1 - b2)], axis=1))
        if n == 0:
            copies[2].wait()
            copies[3].wait()
        first = dot3((ah[...], al[...]), whole, NT)
        if n == 0:
            copies[4].wait()
            copies[5].wait()
        other = dot3((bh[...], bl[...]), rest, NT)
        for k in range(6):
            source, at = (first, k * 128) if k < 2 else (other, (k - 2) * 128)
            for c in range(2):
                out_ref[pl.ds((2 * n + c) * 6 + k, 128, stride=24), :] = source[at : at + 128, c * 128 : (c + 1) * 128]


def inverse_z_kernel(in_ref, ah_ref, al_ref, bh_ref, bl_ref, out_hbm, out, sems):
    first, other = (ah_ref[...], al_ref[...]), (bh_ref[...], bl_ref[...])
    copies = []
    for n in range(2):

        def columns(ks):
            return jnp.concatenate(
                [
                    jnp.concatenate([in_ref[pl.ds(c * 6 + k, 128, stride=24), :] for k in ks], axis=0).T
                    for c in (2 * n, 2 * n + 1)
                ],
                axis=0,
            )

        rows = slice(n * 256, (n + 1) * 256)
        base = dot3(split(columns((0, 1))), first)
        pair = dot3(split(columns((2, 3, 4, 5))), other)
        real, imag = pair[:, :THIRD], ROOT3 * pair[:, THIRD:]
        low = base - 0.5 * real
        out[rows, 0:THIRD] = base + real
        out[rows, THIRD : 2 * THIRD] = low + imag
        out[rows, 2 * THIRD :] = low - imag
        copies.append(pltpu.make_async_copy(out.at[pl.ds(n * 256, 256)], out_hbm.at[pl.ds(n * 256, 256)], sems.at[n]))
        copies[n].start()
    for copy in copies:
        copy.wait()


def forward_xy_kernel(
    dev_ref, in_ref, taps_ref, tabh_ref, tabl_ref, qxh_ref, qxl_ref, qyh_ref, qyl_ref, spec_ref, stat_ref, lo_ref, hi_ref,
    pad_ref, lam_ref, zlam_ref, weight_ref,
):
    taps = padded_taps(taps_ref, pad_ref)
    table = (tabh_ref[...], tabl_ref[...])
    parts = split(taps)
    cols = dot3(table, parts, NT)
    rows = dot3(parts, table, NT)
    lam_x = cols[0:NX, 0:1] * cols[0:NX, 0:1] + cols[NX:, 0:1] * cols[NX:, 0:1]
    lam_y = rows[1:2, 0:NY] * rows[1:2, 0:NY] + rows[1:2, NY:] * rows[1:2, NY:]
    lam_ref[...] = lam_x[0:128] * lam_y
    lam_edge = lam_x[128:129] * lam_y
    zlam_ref[...] = jnp.broadcast_to(depth_response(dev_ref[0], taps[2:3, :])[2], (8, NY))

    block = lax.broadcasted_iota(jnp.int32, (24, 128), 1) // 32
    right = (qyh_ref[...], qyl_ref[...])
    for part in range(4):
        pieces = [[], []]
        for i in range(part * 4, part * 4 + 4):
            for high in range(2):
                got = [in_ref[(i * 8 + high * 4 + j) * 24 : (i * 8 + high * 4 + j + 1) * 24, :] for j in range(4)]
                pieces[high] += list(swap_blocks(got, block))
        field = jnp.concatenate([jnp.concatenate(p, axis=0) for p in pieces], axis=1)
        field = dot3(split(field), right, NT)
        lo_ref[part * 384 : (part + 1) * 384, :] = field[:, :128]
        hi_ref[part * 384 : (part + 1) * 384, :] = field[:, 128:]

    left = (qxh_ref[...], qxl_ref[...])
    top = lax.broadcasted_iota(jnp.int32, (8, NY), 0) == 0
    edge = jnp.zeros((8, NY), F32)
    edge_row = lax.broadcasted_iota(jnp.int32, (8, NY), 0)
    for k in range(6):
        plane = jnp.concatenate([ref[pl.ds(k, 256, stride=6), :] for ref in (lo_ref, hi_ref)], axis=1)
        spec = dot3(left, split(plane))
        spec_ref[k] = spec
        upper, lower = spec[0:128], spec[128:256]
        upper, lower = upper * upper, lower * lower
        slot = k if k < 2 else 1 + k // 2
        edge = edge + jnp.where(edge_row == slot, lower[0:1, :], 0.0)
        tile = upper[0:8] + jnp.where(top, 0.0, lower[0:8])
        body = upper[8:] + lower[8:]
        if k in (3, 5):
            tile = tile + weight_ref[slot, 0:8, :]
            body = body + weight_ref[slot, 8:, :]
        weight_ref[slot, 0:8, :] = tile
        weight_ref[slot, 8:, :] = body

    zrow = lax.broadcasted_iota(jnp.int32, (8, NY), 0)
    zedge = jnp.where(zrow < 2, zlam_ref[...], jnp.where(zrow == 2, zlam_ref[2:3, :], zlam_ref[4:5, :]))
    edge_lam = lam_edge * zedge

    def sums(*funcs):
        def more(parts, w, l):
            return [part + func(w, l).reshape(-1, 8, NY).sum(axis=0) for part, func in zip(parts, funcs)]

        def plane(slot, parts):
            zlam = zlam_ref[pl.ds(jnp.where(slot < 2, slot, 2 * slot - 2), 1), :]
            for r in range(4):
                parts = more(parts, weight_ref[slot, r * 32 : (r + 1) * 32, :], lam_ref[r * 32 : (r + 1) * 32, :] * zlam)
            return parts

        parts = more([jnp.zeros((8, NY), F32) for _ in funcs], edge, edge_lam)
        return [total(p) for p in lax.fori_loop(0, 4, plane, parts)]

    zero, one, two = sums(lambda w, l: w, lambda w, l: w * l, lambda w, l: w * l * l)
    mean = one / jnp.maximum(zero, TINY)
    tau = two / jnp.maximum(one, TINY)

    def centred(w, l):
        d = l - mean
        return w * d * d

    def tilted(w, l):
        d = l - tau
        return w * l * d * d

    var, tilt = sums(centred, tilted)
    step = tau - mean
    slope = (tilt + one * step * step) / jnp.maximum(var, TINY)
    ratio = var / jnp.maximum(zero, TINY)

    def second(w, l):
        d = (l - slope) * (l - mean) - ratio
        return w * d * d

    (last,) = sums(second)
    lane = lax.broadcasted_iota(jnp.int32, (128, 128), 1)
    packed = jnp.zeros((128, 128), F32)
    for n, value in enumerate((zero, mean, tau, var, slope, ratio, tilt, last, one)):
        packed = jnp.where(lane == n, value, packed)
    stat_ref[...] = packed


def inverse_xy_kernel(
    dev_ref, spec_ref, taps_ref, tabh_ref, tabl_ref, qxh_ref, qxl_ref, qyh_ref, qyl_ref, out_ref,
    pad_ref, lam_ref, real_ref, imag_ref, zlam_ref, ulo_ref, uhi_ref, vlo_ref, vhi_ref,
):
    taps = padded_taps(taps_ref, pad_ref)
    table = (tabh_ref[...], tabl_ref[...])
    parts = split(taps)
    cols = dot3(table, parts, NT)
    rows = dot3(parts, table, NT)
    lam_x = cols[0:NX, 0:1] * cols[0:NX, 0:1] + cols[NX:, 0:1] * cols[NX:, 0:1]
    lam_y = rows[1:2, 0:NY] * rows[1:2, 0:NY] + rows[1:2, NY:] * rows[1:2, NY:]
    lam_ref[...] = lam_x * lam_y
    real, imag, zlam = depth_response(dev_ref[0], taps[2:3, :])
    real_ref[...] = jnp.broadcast_to(real, (8, NY))
    imag_ref[...] = jnp.broadcast_to(imag, (8, NY))
    zlam_ref[...] = jnp.broadcast_to(zlam, (8, NY))
    qt = (qxh_ref[...].astype(F32) + qxl_ref[...].astype(F32)).T
    turned = jnp.concatenate([-qt[:, 128:], qt[:, :128]], axis=1)
    left = split(qt * rows[0:1, 0:NX] + turned * rows[0:1, NX:])
    q = qyh_ref[...].astype(F32) + qyl_ref[...].astype(F32)
    turned = jnp.concatenate([-q[128:, :], q[:128, :]], axis=0)
    right = split(q * cols[0:NY, 1:2] + turned * cols[NY:, 1:2])

    refs = (ulo_ref, uhi_ref, vlo_ref, vhi_ref)
    for p in range(3):
        e, o = 2 * p, 2 * p + 1
        a, b = spec_ref[e], spec_ref[o]
        lam = lam_ref[...]
        la, lb = a * (lam * zlam_ref[e : e + 1, :]), b * (lam * zlam_ref[o : o + 1, :])
        for k, x, y, lx, ly in ((e, a, b, la, lb), (o, b, a, lb, la)):
            re, im = real_ref[k : k + 1, :], imag_ref[k : k + 1, :]
            both = jnp.concatenate([re * x + im * y, re * lx + im * ly], axis=1)
            back = dot3(left, split(both))
            for n, ref in enumerate(refs):
                ref[pl.ds(k, 256, stride=6), :] = back[:, n * 128 : (n + 1) * 128]

    block = lax.broadcasted_iota(jnp.int32, (24, 128), 1) // 32
    for which, (lo, hi) in enumerate((refs[0:2], refs[2:4])):
        for part in range(4):
            field = jnp.concatenate([ref[part * 384 : (part + 1) * 384, :] for ref in (lo, hi)], axis=1)
            field = dot3(split(field), right)
            for i in range(4):
                for high in range(2):
                    got = [
                        field[(i * 4 + r) * 24 : (i * 4 + r + 1) * 24, high * 128 : (high + 1) * 128] for r in range(4)
                    ]
                    for j, piece in enumerate(swap_blocks(got, block)):
                        at = ((part * 4 + i) * 8 + high * 4 + j) * 24
                        out_ref[which, at : at + 24, :] = piece


def weights_of(stats):
    zero, mean, tau, var, slope, ratio, tilt, last, one = [stats[n : n + 1, :] for n in range(9)]

    def add(x):
        return jnp.sum(x, axis=1, keepdims=True)

    all_zero = add(zero)
    all_mean = add(one) / all_zero
    shift = mean - all_mean
    all_var = add(var + shift * shift * zero)
    all_ratio = all_var / all_zero
    lean = tau - all_mean
    all_slope = add(tilt + one * lean * lean) / all_var
    lean = tau - all_mean - all_var / (all_zero * all_mean)
    all_tilt = add(tilt + one * lean * lean)
    first = shift + (slope - all_slope)
    const = shift * (mean - all_slope) + ratio - all_ratio
    all_last = add(last + first * first * var + const * const * zero)

    beta_one = jnp.sqrt(all_zero)
    alpha_one = jnp.sqrt(all_mean)
    beta_two = jnp.sqrt(all_var / (all_zero * all_mean))
    alpha_two = jnp.sqrt(all_tilt / all_var)
    beta_three = jnp.sqrt(all_last / all_tilt)

    gram_aa = alpha_one * alpha_one + beta_two * beta_two
    gram_ab = beta_two * alpha_two
    gram_bb = alpha_two * alpha_two + beta_three * beta_three
    target = alpha_one * beta_one
    lane = lax.broadcasted_iota(jnp.int32, (1, 128), 1)
    log_grid = (jnp.minimum(lane, 15).astype(F32) * 0.2 - 3.0) * float(np.log(10.0))
    lambdas = alpha_one * jnp.exp(log_grid)

    def project(squared):
        entry_a = gram_aa + squared
        entry_b = gram_bb + squared
        determ = entry_a * entry_b - gram_ab * gram_ab
        return (entry_b * target / determ, -gram_ab * target / determ, entry_a, entry_b, determ)

    coef_one, coef_two, entry_a, entry_b, determ = project(lambdas * lambdas)
    miss_one = beta_one - alpha_one * coef_one
    miss_two = -(beta_two * coef_one + alpha_two * coef_two)
    miss_three = -beta_three * coef_two
    trace_sum = (entry_b * gram_aa - 2.0 * gram_ab * gram_ab + entry_a * gram_bb) / determ
    left = 3.0 - trace_sum
    scores = (
        3.0
        * (miss_one * miss_one + miss_two * miss_two + miss_three * miss_three)
        / (left * left * beta_one * beta_one)
    )
    shifted = scores + 0.05
    shifted = shifted * shifted
    weights = jnp.where(lane < 16, 1.0 / (shifted * shifted), 0.0)
    chosen = jnp.exp(add(weights * jnp.log(lambdas)) / add(weights))
    coef_one, coef_two, entry_a, entry_b, determ = project(chosen * chosen)
    scale = 1.0 / (alpha_one * beta_one)
    lead = coef_two / alpha_two
    c2 = lead * scale / beta_two
    c1 = coef_one * scale - lead * (alpha_one / (beta_one * beta_two) + beta_two * scale)
    return c1, c2


def combine_kernel(stat_ref, both_ref, out_ref):
    c1, c2 = weights_of(stat_ref[...].T)
    c1, c2 = jnp.broadcast_to(c1, (8, 128)), jnp.broadcast_to(c2, (8, 128))
    for n in range(384):
        at = slice(n * 8, n * 8 + 8)
        out_ref[at, :] = c1 * both_ref[0, at, :] + c2 * both_ref[1, at, :]


def sds(shape, dtype=F32):
    return jax.ShapeDtypeStruct(shape, dtype)


def make_local():
    vmem = pl.BlockSpec(memory_space=pltpu.VMEM)
    smem = pl.BlockSpec(memory_space=pltpu.SMEM)
    hbm = pl.BlockSpec(memory_space=pltpu.HBM)
    params = pltpu.CompilerParams(vmem_limit_bytes=48 << 20)

    first, other = depth_basis()
    depth = (*halves(first), *halves(other))
    basis = plane_basis(NX)
    place = np.arange(NX)
    qx = halves(basis[:, 16 * (place // 16) + 4 * (place % 4) + (place // 4) % 4])
    qy = halves(basis)
    table = halves(plane_table(NX))
    half_rows = pltpu.VMEM((1536, 128), F32)
    tile = pltpu.VMEM((8, NY), F32)

    def exchange(chunks):
        return lax.all_to_all(chunks, ("gx", "gy"), 0, 0, tiled=True)

    def local(observed, psf_taps):
        dev = (lax.axis_index("gx") * 8 + lax.axis_index("gy")).astype(jnp.int32).reshape(1)
        sent = pl.pallas_call(
            forward_z_kernel,
            in_specs=[hbm] * 5,
            out_specs=vmem,
            out_shape=sds((3072, 128)),
            scratch_shapes=[pltpu.VMEM((512, NZ), F32)]
            + [pltpu.VMEM((THIRD, THIRD), BF16)] * 2
            + [pltpu.VMEM((2 * THIRD, 2 * THIRD), BF16)] * 2
            + [pltpu.SemaphoreType.DMA((6,))],
            compiler_params=params,
            name="forward_z",
        )(observed.reshape(512, NZ), *depth)
        got = exchange(sent.reshape(128, 24, 128)).reshape(3072, 128)
        spec, stat = pl.pallas_call(
            forward_xy_kernel,
            in_specs=[smem] + [vmem] * 8,
            out_specs=[vmem] * 2,
            out_shape=[sds((6, NX, NY)), sds((128, 128))],
            scratch_shapes=[half_rows] * 2
            + [pltpu.VMEM((8, 128), F32), pltpu.VMEM((128, NY), F32), tile, pltpu.VMEM((4, 128, NY), F32)],
            compiler_params=params,
            name="forward_xy",
        )(dev, got, psf_taps, *table, *qx, *qy)
        stats = exchange(stat.reshape(128, 1, 128)).reshape(128, 128)
        both = pl.pallas_call(
            inverse_xy_kernel,
            in_specs=[smem] + [vmem] * 8,
            out_specs=vmem,
            out_shape=sds((2, 3072, 128)),
            scratch_shapes=[pltpu.VMEM((8, 128), F32), pltpu.VMEM((NX, NY), F32)] + [tile] * 3 + [half_rows] * 4,
            compiler_params=params,
            name="inverse_xy",
        )(dev, spec, psf_taps, *table, *qx, *qy)
        sent = pl.pallas_call(
            combine_kernel,
            in_specs=[vmem] * 2,
            out_specs=vmem,
            out_shape=sds((3072, 128)),
            compiler_params=params,
            name="combine",
        )(stats, both)
        got = exchange(sent.reshape(128, 24, 128)).reshape(3072, 128)
        out = pl.pallas_call(
            inverse_z_kernel,
            in_specs=[vmem] * 5,
            out_specs=hbm,
            out_shape=sds((512, NZ)),
            scratch_shapes=[pltpu.VMEM((512, NZ), F32), pltpu.SemaphoreType.DMA((2,))],
            compiler_params=params,
            name="inverse_z",
        )(got, *depth)
        return out.reshape(16, 32, NZ)

    return local


def solution(mesh):
    in_specs = (P("gx", "gy", None), P())
    out_specs = P("gx", "gy", None)
    return jax.shard_map(make_local(), mesh=mesh, in_specs=in_specs, out_specs=out_specs, check_vma=False)
```

```python
import jax
import jax.numpy as jnp
import numpy as np
from jax import lax
from jax.experimental import pallas as pl
from jax.experimental.pallas import tpu as pltpu
from jax.sharding import PartitionSpec as P

NX, NY, NZ, TAPS = 256, 256, 768, 31
HALF = TAPS // 2
THIRD = NZ // 3
ROOT3 = float(np.sqrt(3.0) / 2.0)
F32, BF16 = jnp.float32, jnp.bfloat16
TINY = 1e-30
NN = ((1,), (0,))
NT = ((1,), (1,))


def halves(values):
    hi = np.asarray(values, np.float32).astype(BF16)
    lo = (values - hi.astype(np.float64)).astype(np.float32).astype(BF16)
    return hi, lo


def plane_basis(n):
    pos = np.arange(n)
    freq = np.arange(n // 2)[:, None]
    angle = 2.0 * np.pi * ((freq * pos) % n) / n
    basis = np.concatenate([np.cos(angle), np.sin(angle)]) * np.sqrt(2.0 / n)
    basis[0] = 1.0 / np.sqrt(n)
    basis[n // 2] = np.where(pos % 2 == 0, 1.0, -1.0) / np.sqrt(n)
    return basis


def plane_table(n):
    freq = np.arange(n) % (n // 2)
    freq[n // 2] = n // 2
    offset = np.arange(TAPS) - HALF
    turn = (freq[:, None] * offset) % n
    sine = np.where(turn % (n // 2) == 0, 0.0, np.sin(2.0 * np.pi * turn / n))
    table = np.zeros((2 * n, 128))
    table[:n, :TAPS] = np.cos(2.0 * np.pi * turn / n)
    table[n:, :TAPS] = sine
    return table


def depth_basis():
    pos = np.arange(THIRD)
    dev = np.arange(128)[:, None]
    scale = np.sqrt(2.0 / NZ)

    def angle(freq):
        return 2.0 * np.pi * ((freq * pos) % NZ) / NZ

    cos0, sin0 = scale * np.cos(angle(3 * dev)), scale * np.sin(angle(3 * dev))
    cos0[0] = 1.0 / np.sqrt(NZ)
    sin0[0] = np.where(pos % 2 == 0, 1.0, -1.0) / np.sqrt(NZ)
    first = np.concatenate([cos0, sin0])
    rest = []
    for step, sign in ((1, 1.0), (2, -1.0)):
        cos, sin = scale * np.cos(angle(3 * dev + step)), scale * np.sin(angle(3 * dev + step))
        rest.append(np.concatenate([cos, -sign * sin], axis=1))
        rest.append(np.concatenate([sin, sign * cos], axis=1))
    return first, np.concatenate(rest)


def split(values):
    hi = values.astype(BF16)
    return hi, (values - hi.astype(F32)).astype(BF16)


def dot3(left, right, dims=NN):
    def one(a, b):
        return lax.dot_general(a, b, (dims, ((), ())), preferred_element_type=F32)

    return one(left[0], right[0]) + (one(left[0], right[1]) + one(left[1], right[0]))


def total(values):
    return jnp.sum(values, axis=(0, 1), keepdims=True)


def depth_response(dev, taps):
    row = lax.broadcasted_iota(jnp.int32, (8, 128), 0)
    offset = lax.broadcasted_iota(jnp.int32, (8, 128), 1).astype(F32) - float(HALF)
    pair = dev * 3 + row // 2
    odd = row % 2
    first = pair == 0
    freq = jnp.where(first & (odd == 1), NZ // 2, pair).astype(F32)
    turn = freq * offset
    turn = turn - float(NZ) * jnp.floor(turn * (1.0 / NZ))
    angle = turn * (2.0 * np.pi / NZ)
    real = jnp.sum(jnp.cos(angle) * taps, axis=1, keepdims=True)
    imag = jnp.sum(jnp.where(first, 0.0, jnp.sin(angle)) * taps, axis=1, keepdims=True)
    return real, jnp.where(odd[:, 0:1] == 1, -imag, imag), real * real + imag * imag


def swap_blocks(vecs):
    block = lax.broadcasted_iota(jnp.int32, vecs[0].shape, 1) // 32
    odd, high = (block & 1) != 0, (block & 2) != 0

    def pick(arrays, first):
        pairs = [jnp.where(odd, arrays[(n + 1) % 4], arrays[n]) for n in range(4)]
        return [jnp.where(high, pairs[(n + 2) % 4], pairs[n % 4]) for n in first]

    turned = [pltpu.roll(v, 32 * n, 1) if n else v for n, v in enumerate(pick(vecs, range(4)))]
    return pick(turned, (0, 3, 2, 1))


def taps_kernel(
    dev_ref, taps_ref, tabh_ref, tabl_ref, qxh_ref, qxl_ref, qyh_ref, qyl_ref, lam_ref, zed_ref, lam2_ref, zed2_ref,
    mxh_ref, mxl_ref, myh_ref, myl_ref, pad_ref,
):
    pad_ref[...] = jnp.zeros((8, 128), F32)
    pad_ref[0:3, 0:TAPS] = taps_ref[...]
    taps = pad_ref[...]
    table = (tabh_ref[...], tabl_ref[...])
    parts = split(taps)
    cols = dot3(table, parts, NT)
    rows = dot3(parts, table, NT)
    lam_x = cols[0:NX, 0:1] * cols[0:NX, 0:1] + cols[NX:, 0:1] * cols[NX:, 0:1]
    lam_y = rows[1:2, 0:NY] * rows[1:2, 0:NY] + rows[1:2, NY:] * rows[1:2, NY:]
    lam_ref[...] = lam_x * lam_y
    lam2_ref[...] = lam_x * lam_y
    for n, value in enumerate(depth_response(dev_ref[0], taps[2:3, :])):
        zed_ref[n * 8 : n * 8 + 8, :] = jnp.broadcast_to(value, (8, NY))
        zed2_ref[n * 8 : n * 8 + 8, :] = jnp.broadcast_to(value, (8, NY))
    qt = (qxh_ref[...].astype(F32) + qxl_ref[...].astype(F32)).T
    turned = jnp.concatenate([-qt[:, 128:], qt[:, :128]], axis=1)
    mxh_ref[...], mxl_ref[...] = split(qt * rows[0:1, 0:NX] + turned * rows[0:1, NX:])
    q = (qyh_ref[...].astype(F32) + qyl_ref[...].astype(F32)).T
    turned = jnp.concatenate([-q[128:, :], q[:128, :]], axis=0)
    myh_ref[...], myl_ref[...] = split(q * cols[0:NY, 1:2] + turned * cols[NY:, 1:2])


def forward_z_kernel(
    cells_hbm, ah_hbm, al_hbm, bh_hbm, bl_hbm, out_ref, cells, ah, al, bh, bl, wh, wl, rh, rl, sems
):
    def rows(n):
        return pl.ds(n * 256, 256)

    pairs = [(cells_hbm.at[rows(0)], cells.at[rows(0)]), (ah_hbm, ah), (al_hbm, al), (bh_hbm, bh), (bl_hbm, bl)]
    pairs += [(cells_hbm.at[rows(1)], cells.at[rows(1)])]
    copies = [pltpu.make_async_copy(src, dst, sems.at[n]) for n, (src, dst) in enumerate(pairs)]
    for copy in copies:
        copy.start()

    def prepare(n):
        b0, b1, b2 = [cells[n * 256 : (n + 1) * 256, m * THIRD : (m + 1) * THIRD] for m in range(3)]
        both = b1 + b2
        wh[n], wl[n] = split(b0 + both)
        rh[n, :, 0:THIRD], rl[n, :, 0:THIRD] = split(b0 - 0.5 * both)
        rh[n, :, THIRD:], rl[n, :, THIRD:] = split(ROOT3 * (b1 - b2))

    copies[0].wait()
    prepare(0)
    for copy in copies[1:]:
        copy.wait()
    first, other = (ah[...], al[...]), (bh[...], bl[...])
    for n in range(2):
        if n == 1:
            prepare(1)
        for ks, freqs in (((0, 1), dot3(first, (wh[n], wl[n]), NT)), ((2, 3, 4, 5), dot3(other, (rh[n], rl[n]), NT))):
            for at, k in enumerate(ks):
                for c in range(2):
                    out_ref[pl.ds((2 * n + c) * 6 + k, 128, stride=24), :] = freqs[
                        at * 128 : (at + 1) * 128, c * 128 : (c + 1) * 128
                    ]


def inverse_z_kernel(in_ref, ah_ref, al_ref, bh_ref, bl_ref, out_hbm, out, sems):
    first, other = (ah_ref[...], al_ref[...]), (bh_ref[...], bl_ref[...])
    copies = []
    for n in range(2):

        def columns(ks):
            return jnp.concatenate(
                [
                    jnp.concatenate([in_ref[pl.ds(c * 6 + k, 128, stride=24), :] for k in ks], axis=0).T
                    for c in (2 * n, 2 * n + 1)
                ],
                axis=0,
            )

        rows = slice(n * 256, (n + 1) * 256)
        base = dot3(split(columns((0, 1))), first)
        pair = dot3(split(columns((2, 3, 4, 5))), other)
        real, imag = pair[:, :THIRD], ROOT3 * pair[:, THIRD:]
        low = base - 0.5 * real
        out[rows, 0:THIRD] = base + real
        out[rows, THIRD : 2 * THIRD] = low + imag
        out[rows, 2 * THIRD :] = low - imag
        copies.append(pltpu.make_async_copy(out.at[pl.ds(n * 256, 256)], out_hbm.at[pl.ds(n * 256, 256)], sems.at[n]))
        copies[n].start()
    for copy in copies:
        copy.wait()


def forward_xy_kernel(
    in_ref, lam_all_ref, zed_ref, qxh_ref, qxl_ref, qyh_ref, qyl_ref, spec_hbm, stat_ref, lo_ref, hi_ref, weight_ref,
    spec_ref, sems,
):
    lam_ref = lam_all_ref.at[0:128]
    zlam_ref = zed_ref.at[16:24]
    lam_edge = lam_all_ref[128:129, :]

    right = (qyh_ref[...], qyl_ref[...])
    for part in range(2):
        pieces = [[], []]
        for i in range(part * 8, part * 8 + 8):
            for high in range(2):
                got = [in_ref[(i * 8 + high * 4 + j) * 24 : (i * 8 + high * 4 + j + 1) * 24, :] for j in range(4)]
                pieces[high] += swap_blocks(got)
        field = jnp.concatenate([jnp.concatenate(p, axis=0) for p in pieces], axis=1)
        field = dot3(split(field), right)
        lo_ref[part * 768 : (part + 1) * 768, :] = field[:, :128]
        hi_ref[part * 768 : (part + 1) * 768, :] = field[:, 128:]

    left = (qxh_ref[...], qxl_ref[...])
    copies = []
    top = lax.broadcasted_iota(jnp.int32, (8, NY), 0) == 0
    edge = jnp.zeros((8, NY), F32)
    edge_row = lax.broadcasted_iota(jnp.int32, (8, NY), 0)
    for k in range(6):
        plane = jnp.concatenate([ref[pl.ds(k, 256, stride=6), :] for ref in (lo_ref, hi_ref)], axis=1)
        spec = dot3(left, split(plane))
        spec_ref[k] = spec
        copies.append(pltpu.make_async_copy(spec_ref.at[k], spec_hbm.at[k], sems.at[k]))
        copies[k].start()
        upper, lower = spec[0:128], spec[128:256]
        upper, lower = upper * upper, lower * lower
        slot = k if k < 2 else 1 + k // 2
        edge = edge + jnp.where(edge_row == slot, lower[0:1, :], 0.0)
        tile = upper[0:8] + jnp.where(top, 0.0, lower[0:8])
        body = upper[8:] + lower[8:]
        if k in (3, 5):
            tile = tile + weight_ref[slot, 0:8, :]
            body = body + weight_ref[slot, 8:, :]
        weight_ref[slot, 0:8, :] = tile
        weight_ref[slot, 8:, :] = body

    zrow = lax.broadcasted_iota(jnp.int32, (8, NY), 0)
    zedge = jnp.where(zrow < 2, zlam_ref[...], jnp.where(zrow == 2, zlam_ref[2:3, :], zlam_ref[4:5, :]))
    edge_lam = lam_edge * zedge

    def sums(*funcs):
        def more(parts, w, l):
            return [part + func(w, l).reshape(-1, 8, NY).sum(axis=0) for part, func in zip(parts, funcs)]

        def plane(slot, parts):
            zlam = zlam_ref[pl.ds(jnp.where(slot < 2, slot, 2 * slot - 2), 1), :]
            for r in range(4):
                parts = more(parts, weight_ref[slot, r * 32 : (r + 1) * 32, :], lam_ref[r * 32 : (r + 1) * 32, :] * zlam)
            return parts

        parts = more([jnp.zeros((8, NY), F32) for _ in funcs], edge, edge_lam)
        return [total(p) for p in lax.fori_loop(0, 4, plane, parts)]

    zero, one, two = sums(lambda w, l: w, lambda w, l: w * l, lambda w, l: w * l * l)
    mean = one / jnp.maximum(zero, TINY)
    tau = two / jnp.maximum(one, TINY)

    def centred(w, l):
        d = l - mean
        return w * d * d

    def tilted(w, l):
        d = l - tau
        return w * l * d * d

    var, tilt = sums(centred, tilted)
    step = tau - mean
    slope = (tilt + one * step * step) / jnp.maximum(var, TINY)
    ratio = var / jnp.maximum(zero, TINY)

    def second(w, l):
        d = (l - slope) * (l - mean) - ratio
        return w * d * d

    (last,) = sums(second)
    lane = lax.broadcasted_iota(jnp.int32, (128, 128), 1)
    packed = jnp.zeros((128, 128), F32)
    for n, value in enumerate((zero, mean, tau, var, slope, ratio, tilt, last, one)):
        packed = jnp.where(lane == n, value, packed)
    stat_ref[...] = packed
    for copy in copies:
        copy.wait()


def inverse_xy_kernel(
    spec_hbm, lam_hbm, zed_hbm, mxh_hbm, mxl_hbm, myh_hbm, myl_hbm, out_ref, ulo_ref, uhi_ref, vlo_ref, vhi_ref, spec_ref,
    lam_ref, zed_ref, mxh_ref, mxl_ref, myh_ref, myl_ref, sems,
):
    pairs = [(mxh_hbm, mxh_ref), (mxl_hbm, mxl_ref), (lam_hbm, lam_ref), (zed_hbm, zed_ref)]
    pairs += [(spec_hbm.at[pl.ds(2 * p, 2)], spec_ref.at[pl.ds(2 * p, 2)]) for p in range(3)]
    pairs += [(myh_hbm, myh_ref), (myl_hbm, myl_ref)]
    copies = [pltpu.make_async_copy(src, dst, sems.at[n]) for n, (src, dst) in enumerate(pairs)]
    for copy in copies:
        copy.start()
    for copy in copies:
        copy.wait()
    left, right = (mxh_ref[...], mxl_ref[...]), (myh_ref[...], myl_ref[...])
    refs = (ulo_ref, uhi_ref, vlo_ref, vhi_ref)
    for p in range(3):
        e, o = 2 * p, 2 * p + 1
        a, b = spec_ref[e], spec_ref[o]
        lam = lam_ref[...]
        la, lb = a * (lam * zed_ref[16 + e : 17 + e, :]), b * (lam * zed_ref[16 + o : 17 + o, :])
        for k, x, y, lx, ly in ((e, a, b, la, lb), (o, b, a, lb, la)):
            re, im = zed_ref[k : k + 1, :], zed_ref[8 + k : 9 + k, :]
            both = jnp.concatenate([re * x + im * y, re * lx + im * ly], axis=1)
            back = dot3(left, split(both))
            for n, ref in enumerate(refs):
                ref[pl.ds(k, 256, stride=6), :] = back[:, n * 128 : (n + 1) * 128]

    for which, (lo, hi) in enumerate((refs[0:2], refs[2:4])):
        for part in range(2):
            field = jnp.concatenate([ref[part * 768 : (part + 1) * 768, :] for ref in (lo, hi)], axis=1)
            field = dot3(split(field), right)
            for i in range(8):
                for high in range(2):
                    got = [
                        field[(i * 4 + r) * 24 : (i * 4 + r + 1) * 24, high * 128 : (high + 1) * 128] for r in range(4)
                    ]
                    for j, piece in enumerate(swap_blocks(got)):
                        at = ((part * 8 + i) * 8 + high * 4 + j) * 24
                        out_ref[which, at : at + 24, :] = piece


def weights_of(stats):
    zero, mean, tau, var, slope, ratio, tilt, last, one = [stats[n : n + 1, :] for n in range(9)]

    def add(x):
        return jnp.sum(x, axis=1, keepdims=True)

    all_zero = add(zero)
    all_mean = add(one) / all_zero
    shift = mean - all_mean
    all_var = add(var + shift * shift * zero)
    all_ratio = all_var / all_zero
    lean = tau - all_mean
    all_slope = add(tilt + one * lean * lean) / all_var
    lean = tau - all_mean - all_var / (all_zero * all_mean)
    all_tilt = add(tilt + one * lean * lean)
    first = shift + (slope - all_slope)
    const = shift * (mean - all_slope) + ratio - all_ratio
    all_last = add(last + first * first * var + const * const * zero)

    beta_one = jnp.sqrt(all_zero)
    alpha_one = jnp.sqrt(all_mean)
    beta_two = jnp.sqrt(all_var / (all_zero * all_mean))
    alpha_two = jnp.sqrt(all_tilt / all_var)
    beta_three = jnp.sqrt(all_last / all_tilt)

    gram_aa = alpha_one * alpha_one + beta_two * beta_two
    gram_ab = beta_two * alpha_two
    gram_bb = alpha_two * alpha_two + beta_three * beta_three
    target = alpha_one * beta_one
    lane = lax.broadcasted_iota(jnp.int32, (1, 128), 1)
    log_grid = (jnp.minimum(lane, 15).astype(F32) * 0.2 - 3.0) * float(np.log(10.0))
    lambdas = alpha_one * jnp.exp(log_grid)

    def project(squared):
        entry_a = gram_aa + squared
        entry_b = gram_bb + squared
        determ = entry_a * entry_b - gram_ab * gram_ab
        return (entry_b * target / determ, -gram_ab * target / determ, entry_a, entry_b, determ)

    coef_one, coef_two, entry_a, entry_b, determ = project(lambdas * lambdas)
    miss_one = beta_one - alpha_one * coef_one
    miss_two = -(beta_two * coef_one + alpha_two * coef_two)
    miss_three = -beta_three * coef_two
    trace_sum = (entry_b * gram_aa - 2.0 * gram_ab * gram_ab + entry_a * gram_bb) / determ
    left = 3.0 - trace_sum
    scores = (
        3.0
        * (miss_one * miss_one + miss_two * miss_two + miss_three * miss_three)
        / (left * left * beta_one * beta_one)
    )
    shifted = scores + 0.05
    shifted = shifted * shifted
    weights = jnp.where(lane < 16, 1.0 / (shifted * shifted), 0.0)
    chosen = jnp.exp(add(weights * jnp.log(lambdas)) / add(weights))
    coef_one, coef_two, entry_a, entry_b, determ = project(chosen * chosen)
    scale = 1.0 / (alpha_one * beta_one)
    lead = coef_two / alpha_two
    c2 = lead * scale / beta_two
    c1 = coef_one * scale - lead * (alpha_one / (beta_one * beta_two) + beta_two * scale)
    return c1, c2


def combine_kernel(stat_ref, both_ref, out_ref):
    c1, c2 = weights_of(stat_ref[...].T)
    c1, c2 = jnp.broadcast_to(c1, (8, 128)), jnp.broadcast_to(c2, (8, 128))
    for n in range(384):
        at = slice(n * 8, n * 8 + 8)
        out_ref[at, :] = c1 * both_ref[0, at, :] + c2 * both_ref[1, at, :]


def make_local():
    vmem = pl.BlockSpec(memory_space=pltpu.VMEM)
    smem = pl.BlockSpec(memory_space=pltpu.SMEM)
    hbm = pl.BlockSpec(memory_space=pltpu.HBM)
    params = pltpu.CompilerParams(vmem_limit_bytes=40 << 20)

    first, other = depth_basis()
    depth = (*halves(first), *halves(other))
    basis = plane_basis(NX)
    place = np.arange(NX)
    qx = halves(basis[:, 16 * (place // 16) + 4 * (place % 4) + (place // 4) % 4])
    qy = halves(basis.T)
    table = halves(plane_table(NX))
    half_rows = pltpu.VMEM((1536, 128), F32)
    square = pltpu.VMEM((NX, NX), BF16)
    planes = pltpu.VMEM((6, NX, NY), F32)

    def exchange(chunks):
        return lax.all_to_all(chunks, ("gx", "gy"), 0, 0, tiled=True)

    def in_hbm(*arrays):
        return [pltpu.with_memory_space_constraint(x, pltpu.HBM) for x in arrays]

    def local(observed, psf_taps):
        dev = (lax.axis_index("gx") * 8 + lax.axis_index("gy")).astype(jnp.int32).reshape(1)
        sent = pl.pallas_call(
            forward_z_kernel,
            in_specs=[hbm] * 5,
            out_specs=vmem,
            out_shape=pltpu.VMEM((3072, 128), F32),
            scratch_shapes=[pltpu.VMEM((512, NZ), F32)]
            + [pltpu.VMEM((THIRD, THIRD), BF16)] * 2
            + [pltpu.VMEM((2 * THIRD, 2 * THIRD), BF16)] * 2
            + [pltpu.VMEM((2, 256, THIRD), BF16)] * 2
            + [pltpu.VMEM((2, 256, 2 * THIRD), BF16)] * 2
            + [pltpu.SemaphoreType.DMA((6,))],
            compiler_params=params,
            name="forward_z",
        )(*in_hbm(observed.reshape(512, NZ), *(jnp.asarray(x) for x in depth)))
        lam, zed, *back = pl.pallas_call(
            taps_kernel,
            in_specs=[smem] + [vmem] * 7,
            out_specs=[vmem] * 8,
            out_shape=[space(shape, F32) for space in (pltpu.VMEM, pltpu.HBM) for shape in ((NX, NY), (24, NY))]
            + [pltpu.HBM((NX, NX), BF16)] * 4,
            scratch_shapes=[pltpu.VMEM((8, 128), F32)],
            name="taps_kernel",
        )(dev, psf_taps, *table, *qx, *qy)
        got = exchange(sent.reshape(128, 24, 128)).reshape(3072, 128)
        spec, stat = pl.pallas_call(
            forward_xy_kernel,
            in_specs=[vmem] * 7,
            out_specs=[hbm, vmem],
            out_shape=[pltpu.HBM((6, NX, NY), F32), jax.ShapeDtypeStruct((128, 128), F32)],
            scratch_shapes=[half_rows] * 2
            + [pltpu.VMEM((4, 128, NY), F32), planes, pltpu.SemaphoreType.DMA((6,))],
            compiler_params=params,
            name="forward_xy",
        )(got, lam, zed, *qx, *qy)
        stats = exchange(stat.reshape(128, 1, 128)).reshape(128, 128)
        both = pl.pallas_call(
            inverse_xy_kernel,
            in_specs=[hbm] * 7,
            out_specs=vmem,
            out_shape=pltpu.VMEM((2, 3072, 128), F32),
            scratch_shapes=[half_rows] * 4
            + [planes, pltpu.VMEM((NX, NY), F32), pltpu.VMEM((24, NY), F32)]
            + [square] * 4
            + [pltpu.SemaphoreType.DMA((9,))],
            compiler_params=params,
            name="inverse_xy",
        )(*in_hbm(spec, *back))
        sent = pl.pallas_call(
            combine_kernel,
            in_specs=[vmem] * 2,
            out_specs=vmem,
            out_shape=pltpu.VMEM((3072, 128), F32),
            compiler_params=params,
            name="combine",
        )(stats, both)
        got = exchange(sent.reshape(128, 24, 128)).reshape(3072, 128)
        out = pl.pallas_call(
            inverse_z_kernel,
            in_specs=[vmem] * 5,
            out_specs=hbm,
            out_shape=jax.ShapeDtypeStruct((512, NZ), F32),
            scratch_shapes=[pltpu.VMEM((512, NZ), F32), pltpu.SemaphoreType.DMA((2,))],
            compiler_params=params,
            name="inverse_z",
        )(got, *depth)
        return out.reshape(16, 32, NZ)

    return local


def solution(mesh):
    in_specs = (P("gx", "gy", None), P())
    out_specs = P("gx", "gy", None)
    return jax.shard_map(make_local(), mesh=mesh, in_specs=in_specs, out_specs=out_specs, check_vma=False)
```

```python
import jax
import jax.numpy as jnp
import numpy as np
from jax import lax
from jax.experimental import pallas as pl
from jax.experimental.pallas import tpu as pltpu
from jax.sharding import PartitionSpec as P

NX, NY, NZ, TAPS = 256, 256, 768, 31
HALF = TAPS // 2
THIRD = NZ // 3
ROOT3 = float(np.sqrt(3.0) / 2.0)
F32, BF16 = jnp.float32, jnp.bfloat16
TINY = 1e-30
NN = ((1,), (0,))
NT = ((1,), (1,))


def halves(values):
    hi = np.asarray(values, np.float32).astype(BF16)
    lo = (values - hi.astype(np.float64)).astype(np.float32).astype(BF16)
    return hi, lo


def plane_basis(n):
    pos = np.arange(n)
    freq = np.arange(n // 2)[:, None]
    angle = 2.0 * np.pi * ((freq * pos) % n) / n
    basis = np.concatenate([np.cos(angle), np.sin(angle)]) * np.sqrt(2.0 / n)
    basis[0] = 1.0 / np.sqrt(n)
    basis[n // 2] = np.where(pos % 2 == 0, 1.0, -1.0) / np.sqrt(n)
    return basis


def plane_table(n):
    freq = np.arange(n) % (n // 2)
    freq[n // 2] = n // 2
    turn = ((np.arange(TAPS) - HALF)[:, None] * freq) % n
    table = np.zeros((32, 2 * n))
    table[:TAPS, :n] = np.cos(2.0 * np.pi * turn / n)
    table[:TAPS, n:] = np.where(turn % (n // 2) == 0, 0.0, np.sin(2.0 * np.pi * turn / n))
    return table


def depth_basis():
    pos = np.arange(THIRD)
    dev = np.arange(128)[:, None]
    blocks = []
    for step in range(3):
        angle = 2.0 * np.pi * (((3 * dev + step) * pos) % NZ) / NZ
        blocks += [np.sqrt(2.0 / NZ) * np.cos(angle), np.sqrt(2.0 / NZ) * np.sin(angle)]
    blocks[0][0] = 1.0 / np.sqrt(NZ)
    blocks[1][0] = np.where(pos % 2 == 0, 1.0, -1.0) / np.sqrt(NZ)
    return np.concatenate(blocks)


def split(values):
    hi = values.astype(BF16)
    return hi, (values - hi.astype(F32)).astype(BF16)


def dot3(left, right, dims=NN):
    def one(a, b):
        return lax.dot_general(a, b, (dims, ((), ())), preferred_element_type=F32)

    return one(left[0], right[0]) + (one(left[0], right[1]) + one(left[1], right[0]))


def total(values):
    return jnp.sum(values, axis=(0, 1), keepdims=True)


def depth_response(dev, taps):
    row = lax.broadcasted_iota(jnp.int32, (8, 128), 0)
    offset = lax.broadcasted_iota(jnp.int32, (8, 128), 1).astype(F32) - float(HALF)
    pair = dev * 3 + row // 2
    odd = row % 2
    first = pair == 0
    freq = jnp.where(first & (odd == 1), NZ // 2, pair).astype(F32)
    turn = freq * offset
    turn = turn - float(NZ) * jnp.floor(turn * (1.0 / NZ))
    angle = turn * (2.0 * np.pi / NZ)
    real = jnp.sum(jnp.cos(angle) * taps, axis=1, keepdims=True)
    imag = jnp.sum(jnp.where(first, 0.0, jnp.sin(angle)) * taps, axis=1, keepdims=True)
    return real, jnp.where(odd[:, 0:1] == 1, -imag, imag), real * real + imag * imag


def swap_blocks(vecs):
    block = lax.broadcasted_iota(jnp.int32, vecs[0].shape, 1) // 32
    odd, high = (block & 1) != 0, (block & 2) != 0

    def pick(arrays, first):
        pairs = [jnp.where(odd, arrays[(n + 1) % 4], arrays[n]) for n in range(4)]
        return [jnp.where(high, pairs[(n + 2) % 4], pairs[n % 4]) for n in first]

    turned = [pltpu.roll(v, 32 * n, 1) if n else v for n, v in enumerate(pick(vecs, range(4)))]
    return pick(turned, (0, 3, 2, 1))


def plane_response(taps_ref, pad_ref, table):
    pad_ref[...] = jnp.zeros((8, 128), F32)
    pad_ref[0:3, 0:TAPS] = taps_ref[...]
    taps = pad_ref[...]
    rows = dot3(split(taps[:, 0:32]), table)
    cols = rows.T
    lam_x = cols[0:NX, 0:1] * cols[0:NX, 0:1] + cols[NX:, 0:1] * cols[NX:, 0:1]
    lam_y = rows[1:2, 0:NY] * rows[1:2, 0:NY] + rows[1:2, NY:] * rows[1:2, NY:]
    return taps, rows, cols, lam_x, lam_y


def forward_z_kernel(dev_ref, cells_hbm, fh_hbm, fl_hbm, out_ref, cells, fh, fl, half, wide, sems):
    parts = [(cells_hbm, cells, 0), (fh_hbm, fh, 0), (fl_hbm, fl, 0), (fh_hbm, fh, 1), (fl_hbm, fl, 1)]
    parts += [(fh_hbm, fh, 2), (fl_hbm, fl, 2), (cells_hbm, cells, 1)]
    copies = []
    for n, (src, dst, block) in enumerate(parts):
        rows = pl.ds(block * 256, 256)
        copies.append(pltpu.make_async_copy(src.at[rows], dst.at[rows], sems.at[n]))
        copies[n].start()

    def prepare(n):
        b0, b1, b2 = [cells[n * 256 : (n + 1) * 256, m * THIRD : (m + 1) * THIRD] for m in range(3)]
        both = b1 + b2
        for at, value in enumerate((b0 + both, b0 - 0.5 * both, ROOT3 * (b1 - b2))):
            half[n, at], wide[n, at] = split(value)

    def store(freqs, p, n):
        for par in range(2):
            for c in range(2):
                out_ref[pl.ds(p * 8 + (2 * n + c) * 2 + par, 128, stride=24), :] = freqs[par][:, c * 128 : (c + 1) * 128]

    def transform(p, n):
        basis = (fh[p * 256 : (p + 1) * 256, :], fl[p * 256 : (p + 1) * 256, :])

        def one(at):
            return dot3(basis, (half[n, at], wide[n, at]), NT)

        if p == 0:
            whole = one(0)
            store((whole[0:128], whole[128:]), p, n)
        else:
            real, imag = one(1), one(2)
            if p == 1:
                store((real[0:128] - imag[128:], real[128:] + imag[0:128]), p, n)
            else:
                store((real[0:128] + imag[128:], real[128:] - imag[0:128]), p, n)

    copies[0].wait()
    prepare(0)
    for copy in copies[1:5]:
        copy.wait()
    transform(0, 0)
    transform(1, 0)
    for copy in copies[5:]:
        copy.wait()
    transform(2, 0)
    prepare(1)
    for p in range(3):
        transform(p, 1)


def inverse_z_kernel(in_ref, fh_ref, fl_ref, out_hbm, out, sems):
    base_f = (fh_ref[0:256, :], fl_ref[0:256, :])
    pair_f = (fh_ref[256:, :], fl_ref[256:, :])
    copies = []
    for n in range(2):

        def columns(*ks):
            blocks = []
            for c in (2 * n, 2 * n + 1):
                got = [in_ref[pl.ds(abs(k) // 2 * 8 + c * 2 + abs(k) % 2, 128, stride=24), :].T for k in ks]
                blocks.append(jnp.concatenate(got, axis=1))
            return split(jnp.concatenate(blocks, axis=0))

        base = dot3(columns(0, 1), base_f)
        hi, lo = columns(2, 3, 4, 5)
        real = dot3((hi, lo), pair_f)

        def turned(x):
            y2, y3, y4, y5 = [x[:, at * 128 : (at + 1) * 128] for at in range(4)]
            return jnp.concatenate([y3, -y2, -y5, y4], axis=1)

        imag = ROOT3 * dot3((turned(hi), turned(lo)), pair_f)
        low = base - 0.5 * real
        for q in range(2):
            rows = slice(q * 128, (q + 1) * 128)
            at = n * 256 + q * 128
            out[at : at + 128, 0:THIRD] = base[rows] + real[rows]
            out[at : at + 128, THIRD : 2 * THIRD] = low[rows] + imag[rows]
            out[at : at + 128, 2 * THIRD :] = low[rows] - imag[rows]
            here = pl.ds(at, 128)
            copies.append(pltpu.make_async_copy(out.at[here], out_hbm.at[here], sems.at[2 * n + q]))
            copies[-1].start()
    for copy in copies:
        copy.wait()


def forward_xy_kernel(
    dev_ref, in_ref, taps_ref, tabh_ref, tabl_ref, qxh_ref, qxl_ref, qyh_ref, qyl_ref, spec_hbm, stat_ref, fh_ref, fl_ref,
    lo_ref, hi_ref, weight_ref, spec_ref, pad_ref, lam_ref, zlam_ref, sems,
):
    taps, rows, cols, lam_x, lam_y = plane_response(taps_ref, pad_ref, (tabh_ref[...], tabl_ref[...]))
    lam_ref[...] = lam_x[0:128] * lam_y
    lam_edge = lam_x[128:129] * lam_y
    zlam_ref[...] = jnp.broadcast_to(depth_response(dev_ref[0], taps[2:3, :])[2], (8, NY))
    left, right = (qxh_ref[...], qxl_ref[...]), (qyh_ref[...], qyl_ref[...])
    copies = []

    def gather(p):
        for i in range(16):
            for high in range(2):
                first = [(i * 8 + high * 4 + j) * 24 + p * 8 for j in range(4)]
                got = swap_blocks([in_ref[at : at + 8, :] for at in first])
                for r in (0, 2):
                    at = slice((i * 4 + r) * 8, (i * 4 + r + 2) * 8)
                    lanes = slice(high * 128, (high + 1) * 128)
                    fh_ref[p, at, lanes], fl_ref[p, at, lanes] = split(jnp.concatenate(got[r : r + 2], axis=0))

    def along_y(p):
        for h in range(2):
            at = slice(h * 256, (h + 1) * 256)
            field = dot3((fh_ref[p, at], fl_ref[p, at]), right)
            at = slice(p * 512 + h * 256, p * 512 + (h + 1) * 256)
            lo_ref[at, :], hi_ref[at, :] = field[:, :128], field[:, 128:]

    top = lax.broadcasted_iota(jnp.int32, (8, NY), 0) == 0
    edges = []

    def along_x(p):
        specs = []
        for par in range(2):
            plane = [ref[pl.ds(p * 512 + par, 256, stride=2), :] for ref in (lo_ref, hi_ref)]
            specs.append(dot3(left, split(jnp.concatenate(plane, axis=1))))
        tiles, bodies = [], []
        for par, spec in enumerate(specs):
            spec_ref[2 * p + par] = spec
            upper, lower = spec[0:128], spec[128:256]
            upper, lower = upper * upper, lower * lower
            edges.append(lower[0:1, :])
            tiles.append(upper[0:8] + jnp.where(top, 0.0, lower[0:8]))
            bodies.append(upper[8:] + lower[8:])
        if p == 0:
            for par in range(2):
                weight_ref[par, 0:8, :], weight_ref[par, 8:, :] = tiles[par], bodies[par]
        else:
            weight_ref[p + 1, 0:8, :], weight_ref[p + 1, 8:, :] = tiles[0] + tiles[1], bodies[0] + bodies[1]
        here = pl.ds(2 * p, 2)
        copies.append(pltpu.make_async_copy(spec_ref.at[here], spec_hbm.at[here], sems.at[p]))
        copies[p].start()

    gather(0)
    along_y(0)
    gather(1)
    along_x(0)
    along_y(1)
    gather(2)
    along_x(1)
    along_y(2)
    along_x(2)

    row = lax.broadcasted_iota(jnp.int32, (8, NY), 0)
    edge = jnp.zeros((8, NY), F32)
    for slot, value in enumerate((edges[0], edges[1], edges[2] + edges[3], edges[4] + edges[5])):
        edge = jnp.where(row == slot, value, edge)
    zedge = jnp.where(row < 2, zlam_ref[...], jnp.where(row == 2, zlam_ref[2:3, :], zlam_ref[4:5, :]))
    edge_lam = lam_edge * zedge

    def sums(*funcs):
        def more(parts, w, l):
            return [part + func(w, l).reshape(-1, 8, NY).sum(axis=0) for part, func in zip(parts, funcs)]

        def plane(slot, parts):
            zlam = zlam_ref[pl.ds(jnp.where(slot < 2, slot, 2 * slot - 2), 1), :]
            for r in range(4):
                parts = more(parts, weight_ref[slot, r * 32 : (r + 1) * 32, :], lam_ref[r * 32 : (r + 1) * 32, :] * zlam)
            return parts

        parts = more([jnp.zeros((8, NY), F32) for _ in funcs], edge, edge_lam)
        return [total(p) for p in lax.fori_loop(0, 4, plane, parts)]

    zero, one, two = sums(lambda w, l: w, lambda w, l: w * l, lambda w, l: w * l * l)
    mean = one / jnp.maximum(zero, TINY)
    tau = two / jnp.maximum(one, TINY)

    def centred(w, l):
        d = l - mean
        return w * d * d

    def tilted(w, l):
        d = l - tau
        return w * l * d * d

    var, tilt = sums(centred, tilted)
    step = tau - mean
    slope = (tilt + one * step * step) / jnp.maximum(var, TINY)
    ratio = var / jnp.maximum(zero, TINY)

    def second(w, l):
        d = (l - slope) * (l - mean) - ratio
        return w * d * d

    (last,) = sums(second)
    lane = lax.broadcasted_iota(jnp.int32, (128, 128), 1)
    packed = jnp.zeros((128, 128), F32)
    for n, value in enumerate((zero, mean, tau, var, slope, ratio, tilt, last, one)):
        packed = jnp.where(lane == n, value, packed)
    stat_ref[...] = packed
    for copy in copies:
        copy.wait()


def inverse_xy_kernel(
    dev_ref, spec_hbm, taps_hbm, tabh_hbm, tabl_hbm, qxh_hbm, qxl_hbm, qyh_hbm, qyl_hbm, out_ref, ulo_ref, uhi_ref, vlo_ref,
    vhi_ref, spec_ref, taps_ref, tabh_ref, tabl_ref, qxh_ref, qxl_ref, qyh_ref, qyl_ref, pad_ref, lam_ref, zed_ref, sems,
):
    pairs = [(taps_hbm, taps_ref), (tabh_hbm, tabh_ref), (tabl_hbm, tabl_ref), (qxh_hbm, qxh_ref), (qxl_hbm, qxl_ref)]
    pairs += [(qyh_hbm, qyh_ref), (qyl_hbm, qyl_ref), (spec_hbm, spec_ref)]
    copies = [pltpu.make_async_copy(src, dst, sems.at[n]) for n, (src, dst) in enumerate(pairs)]
    for copy in copies:
        copy.start()
    for copy in copies[:7]:
        copy.wait()
    taps, rows, cols, lam_x, lam_y = plane_response(taps_ref, pad_ref, (tabh_ref[...], tabl_ref[...]))
    lam_ref[...] = lam_x * lam_y
    for n, value in enumerate(depth_response(dev_ref[0], taps[2:3, :])):
        zed_ref[n * 8 : n * 8 + 8, :] = jnp.broadcast_to(value, (8, NY))
    qt = (qxh_ref[...].astype(F32) + qxl_ref[...].astype(F32)).T
    turned = jnp.concatenate([-qt[:, 128:], qt[:, :128]], axis=1)
    left = split(qt * rows[0:1, 0:NX] + turned * rows[0:1, NX:])
    q = (qyh_ref[...].astype(F32) + qyl_ref[...].astype(F32)).T
    turned = jnp.concatenate([-q[128:, :], q[:128, :]], axis=0)
    right = split(q * cols[0:NY, 1:2] + turned * cols[NY:, 1:2])
    copies[7].wait()
    refs = (ulo_ref, uhi_ref, vlo_ref, vhi_ref)
    for p in range(3):
        e, o = 2 * p, 2 * p + 1
        a, b = spec_ref[e], spec_ref[o]
        lam = lam_ref[...]
        la, lb = a * (lam * zed_ref[16 + e : 17 + e, :]), b * (lam * zed_ref[16 + o : 17 + o, :])
        for k, x, y, lx, ly in ((e, a, b, la, lb), (o, b, a, lb, la)):
            re, im = zed_ref[k : k + 1, :], zed_ref[8 + k : 9 + k, :]
            both = jnp.concatenate([re * x + im * y, re * lx + im * ly], axis=1)
            back = dot3(left, split(both))
            for n, ref in enumerate(refs):
                ref[pl.ds(p * 512 + k % 2, 256, stride=2), :] = back[:, n * 128 : (n + 1) * 128]

        for which, pair in enumerate((refs[0:2], refs[2:4])):
            field = jnp.concatenate([ref[p * 512 : (p + 1) * 512, :] for ref in pair], axis=1)
            field = dot3(split(field), right)
            for i in range(16):
                for high in range(2):
                    got = [field[(i * 4 + r) * 8 : (i * 4 + r + 1) * 8, high * 128 : (high + 1) * 128] for r in range(4)]
                    for j, piece in enumerate(swap_blocks(got)):
                        at = (i * 8 + high * 4 + j) * 24 + p * 8
                        out_ref[which, at : at + 8, :] = piece


def weights_of(stats):
    zero, mean, tau, var, slope, ratio, tilt, last, one = [stats[n : n + 1, :] for n in range(9)]

    def add(x):
        return jnp.sum(x, axis=1, keepdims=True)

    all_zero = add(zero)
    all_mean = add(one) / all_zero
    shift = mean - all_mean
    all_var = add(var + shift * shift * zero)
    all_ratio = all_var / all_zero
    lean = tau - all_mean
    all_slope = add(tilt + one * lean * lean) / all_var
    lean = tau - all_mean - all_var / (all_zero * all_mean)
    all_tilt = add(tilt + one * lean * lean)
    first = shift + (slope - all_slope)
    const = shift * (mean - all_slope) + ratio - all_ratio
    all_last = add(last + first * first * var + const * const * zero)

    beta_one = jnp.sqrt(all_zero)
    alpha_one = jnp.sqrt(all_mean)
    beta_two = jnp.sqrt(all_var / (all_zero * all_mean))
    alpha_two = jnp.sqrt(all_tilt / all_var)
    beta_three = jnp.sqrt(all_last / all_tilt)

    gram_aa = alpha_one * alpha_one + beta_two * beta_two
    gram_ab = beta_two * alpha_two
    gram_bb = alpha_two * alpha_two + beta_three * beta_three
    target = alpha_one * beta_one
    lane = lax.broadcasted_iota(jnp.int32, (1, 128), 1)
    log_grid = (jnp.minimum(lane, 15).astype(F32) * 0.2 - 3.0) * float(np.log(10.0))
    lambdas = alpha_one * jnp.exp(log_grid)

    def project(squared):
        entry_a = gram_aa + squared
        entry_b = gram_bb + squared
        determ = entry_a * entry_b - gram_ab * gram_ab
        return (entry_b * target / determ, -gram_ab * target / determ, entry_a, entry_b, determ)

    coef_one, coef_two, entry_a, entry_b, determ = project(lambdas * lambdas)
    miss_one = beta_one - alpha_one * coef_one
    miss_two = -(beta_two * coef_one + alpha_two * coef_two)
    miss_three = -beta_three * coef_two
    trace_sum = (entry_b * gram_aa - 2.0 * gram_ab * gram_ab + entry_a * gram_bb) / determ
    left = 3.0 - trace_sum
    scores = (
        3.0
        * (miss_one * miss_one + miss_two * miss_two + miss_three * miss_three)
        / (left * left * beta_one * beta_one)
    )
    shifted = scores + 0.05
    shifted = shifted * shifted
    weights = jnp.where(lane < 16, 1.0 / (shifted * shifted), 0.0)
    chosen = jnp.exp(add(weights * jnp.log(lambdas)) / add(weights))
    coef_one, coef_two, entry_a, entry_b, determ = project(chosen * chosen)
    scale = 1.0 / (alpha_one * beta_one)
    lead = coef_two / alpha_two
    c2 = lead * scale / beta_two
    c1 = coef_one * scale - lead * (alpha_one / (beta_one * beta_two) + beta_two * scale)
    return c1, c2


def combine_kernel(stat_ref, both_ref, out_ref):
    c1, c2 = weights_of(stat_ref[...].T)
    c1, c2 = jnp.broadcast_to(c1, (8, 128)), jnp.broadcast_to(c2, (8, 128))

    def rows(n, carry):
        for t in range(24):
            at = pl.ds(pl.multiple_of(n * 192 + t * 8, 8), 8)
            out_ref[at, :] = c1 * both_ref[0, at, :] + c2 * both_ref[1, at, :]
        return carry

    lax.fori_loop(0, 16, rows, 0)


def make_local():
    vmem = pl.BlockSpec(memory_space=pltpu.VMEM)
    smem = pl.BlockSpec(memory_space=pltpu.SMEM)
    hbm = pl.BlockSpec(memory_space=pltpu.HBM)
    params = pltpu.CompilerParams(vmem_limit_bytes=40 << 20)

    depth = halves(depth_basis())
    basis = plane_basis(NX)
    place = np.arange(NX)
    qx = halves(basis[:, 16 * (place // 16) + 4 * (place % 4) + (place // 4) % 4])
    qy = halves(basis.T)
    table = halves(plane_table(NX))
    half_rows = pltpu.VMEM((1536, 128), F32)
    tile = pltpu.VMEM((8, 128), F32)
    planes = pltpu.VMEM((6, NX, NY), F32)

    def exchange(chunks):
        return lax.all_to_all(chunks, ("gx", "gy"), 0, 0, tiled=True)

    def in_hbm(*arrays):
        return [pltpu.with_memory_space_constraint(jnp.asarray(x), pltpu.HBM) for x in arrays]

    def local(observed, psf_taps):
        dev = (lax.axis_index("gx") * 8 + lax.axis_index("gy")).astype(jnp.int32).reshape(1)
        sent = pl.pallas_call(
            forward_z_kernel,
            in_specs=[smem] + [hbm] * 3,
            out_specs=vmem,
            out_shape=pltpu.VMEM((3072, 128), F32),
            scratch_shapes=[pltpu.VMEM((512, NZ), F32)]
            + [pltpu.VMEM((3 * THIRD, THIRD), BF16)] * 2
            + [pltpu.VMEM((2, 3, 256, THIRD), BF16)] * 2
            + [pltpu.SemaphoreType.DMA((8,))],
            compiler_params=params,
            name="forward_z",
        )(dev, *in_hbm(observed.reshape(512, NZ), *depth))
        got = exchange(sent.reshape(128, 24, 128)).reshape(3072, 128)
        spec, stat = pl.pallas_call(
            forward_xy_kernel,
            in_specs=[smem] + [vmem] * 8,
            out_specs=[hbm, vmem],
            out_shape=[pltpu.HBM((6, NX, NY), F32), jax.ShapeDtypeStruct((128, 128), F32)],
            scratch_shapes=[pltpu.VMEM((3, 512, NY), BF16)] * 2
            + [half_rows] * 2
            + [pltpu.VMEM((4, 128, NY), F32), planes, tile, pltpu.VMEM((128, NY), F32), pltpu.VMEM((8, NY), F32)]
            + [pltpu.SemaphoreType.DMA((3,))],
            compiler_params=params,
            name="forward_xy",
        )(dev, got, psf_taps, *table, *qx, *qy)
        stats = exchange(stat.reshape(128, 1, 128)).reshape(128, 128)
        both = pl.pallas_call(
            inverse_xy_kernel,
            in_specs=[smem] + [hbm] * 8,
            out_specs=vmem,
            out_shape=pltpu.VMEM((2, 3072, 128), F32),
            scratch_shapes=[half_rows] * 4
            + [planes, pltpu.VMEM((3, TAPS), F32)]
            + [pltpu.VMEM((32, 2 * NX), BF16)] * 2
            + [pltpu.VMEM((NX, NX), BF16)] * 4
            + [tile, pltpu.VMEM((NX, NY), F32), pltpu.VMEM((24, NY), F32)]
            + [pltpu.SemaphoreType.DMA((8,))],
            compiler_params=params,
            name="inverse_xy",
        )(dev, *in_hbm(spec, psf_taps, *table, *qx, *qy))
        sent = pl.pallas_call(
            combine_kernel,
            in_specs=[vmem] * 2,
            out_specs=vmem,
            out_shape=pltpu.VMEM((3072, 128), F32),
            compiler_params=params,
            name="combine",
        )(stats, both)
        got = exchange(sent.reshape(128, 24, 128)).reshape(3072, 128)
        out = pl.pallas_call(
            inverse_z_kernel,
            in_specs=[vmem] * 3,
            out_specs=hbm,
            out_shape=jax.ShapeDtypeStruct((512, NZ), F32),
            scratch_shapes=[pltpu.VMEM((512, NZ), F32), pltpu.SemaphoreType.DMA((4,))],
            compiler_params=params,
            name="inverse_z",
        )(got, *depth)
        return out.reshape(16, 32, NZ)

    return local


def solution(mesh):
    in_specs = (P("gx", "gy", None), P())
    out_specs = P("gx", "gy", None)
    return jax.shard_map(make_local(), mesh=mesh, in_specs=in_specs, out_specs=out_specs, check_vma=False)
```

```python
import jax
import jax.numpy as jnp
import numpy as np
from jax import lax
from jax.experimental import pallas as pl
from jax.experimental.pallas import tpu as pltpu
from jax.sharding import PartitionSpec as P

NX, NY, NZ, TAPS = 256, 256, 768, 31
HALF = TAPS // 2
THIRD = NZ // 3
ROOT3 = float(np.sqrt(3.0) / 2.0)
F32, BF16 = jnp.float32, jnp.bfloat16
TINY = 1e-30
NN = ((1,), (0,))
NT = ((1,), (1,))


def halves(values):
    hi = np.asarray(values, np.float32).astype(BF16)
    lo = (values - hi.astype(np.float64)).astype(np.float32).astype(BF16)
    return hi, lo


def plane_basis(n):
    pos = np.arange(n)
    freq = np.arange(n // 2)[:, None]
    angle = 2.0 * np.pi * ((freq * pos) % n) / n
    basis = np.concatenate([np.cos(angle), np.sin(angle)]) * np.sqrt(2.0 / n)
    basis[0] = 1.0 / np.sqrt(n)
    basis[n // 2] = np.where(pos % 2 == 0, 1.0, -1.0) / np.sqrt(n)
    return basis


def plane_table(n):
    freq = np.arange(n) % (n // 2)
    freq[n // 2] = n // 2
    turn = ((np.arange(TAPS) - HALF)[:, None] * freq) % n
    table = np.zeros((32, 2 * n))
    table[:TAPS, :n] = np.cos(2.0 * np.pi * turn / n)
    table[:TAPS, n:] = np.where(turn % (n // 2) == 0, 0.0, np.sin(2.0 * np.pi * turn / n))
    return table


def depth_basis():
    pos = np.arange(THIRD)
    dev = np.arange(128)[:, None]
    blocks = []
    for step in range(3):
        angle = 2.0 * np.pi * (((3 * dev + step) * pos) % NZ) / NZ
        blocks += [np.sqrt(2.0 / NZ) * np.cos(angle), np.sqrt(2.0 / NZ) * np.sin(angle)]
    blocks[0][0] = 1.0 / np.sqrt(NZ)
    blocks[1][0] = np.where(pos % 2 == 0, 1.0, -1.0) / np.sqrt(NZ)
    return np.concatenate(blocks)


def split(values):
    hi = values.astype(BF16)
    return hi, (values - hi.astype(F32)).astype(BF16)


def dot3(left, right, dims=NN):
    def one(a, b):
        return lax.dot_general(a, b, (dims, ((), ())), preferred_element_type=F32)

    return one(left[0], right[0]) + (one(left[0], right[1]) + one(left[1], right[0]))


def lane_total(values):
    return jnp.broadcast_to(jnp.sum(values, axis=1, keepdims=True), (8, 128))


def total(values):
    sums = lane_total(values[:, :128] + values[:, 128:])
    sums = jnp.broadcast_to(jnp.sum(sums, axis=0, keepdims=True), (8, 128))
    return jnp.concatenate([sums, sums], axis=1)


def depth_response(dev, taps):
    row = lax.broadcasted_iota(jnp.int32, (8, 128), 0)
    offset = lax.broadcasted_iota(jnp.int32, (8, 128), 1).astype(F32) - float(HALF)
    pair = dev * 3 + row // 2
    odd = row % 2
    first = pair == 0
    freq = jnp.where(first & (odd == 1), NZ // 2, pair).astype(F32)
    turn = freq * offset
    turn = turn - float(NZ) * jnp.floor(turn * (1.0 / NZ))
    angle = turn * (2.0 * np.pi / NZ)
    real = jnp.sum(jnp.cos(angle) * taps, axis=1, keepdims=True)
    imag = jnp.sum(jnp.where(first, 0.0, jnp.sin(angle)) * taps, axis=1, keepdims=True)
    return real, jnp.where(odd[:, 0:1] == 1, -imag, imag), real * real + imag * imag


def swap_blocks(vecs):
    block = lax.broadcasted_iota(jnp.int32, vecs[0].shape, 1) // 32
    odd, high = (block & 1) != 0, (block & 2) != 0

    def pick(arrays, first):
        pairs = [jnp.where(odd, arrays[(n + 1) % 4], arrays[n]) for n in range(4)]
        return [jnp.where(high, pairs[(n + 2) % 4], pairs[n % 4]) for n in first]

    turned = [pltpu.roll(v, 32 * n, 1) if n else v for n, v in enumerate(pick(vecs, range(4)))]
    return pick(turned, (0, 3, 2, 1))


def plane_response(taps_ref, pad_ref, table):
    pad_ref[...] = jnp.zeros((8, 128), F32)
    pad_ref[0:3, 0:TAPS] = taps_ref[...]
    taps = pad_ref[...]
    rows = dot3(split(taps[:, 0:32]), table)
    cols = rows.T
    lam_x = cols[0:NX, 0:1] * cols[0:NX, 0:1] + cols[NX:, 0:1] * cols[NX:, 0:1]
    lam_y = rows[1:2, 0:NY] * rows[1:2, 0:NY] + rows[1:2, NY:] * rows[1:2, NY:]
    return taps, rows, cols, lam_x, lam_y


def forward_z_kernel(dev_ref, cells_hbm, fh_hbm, fl_hbm, out_ref, cells, fh, fl, half, wide, sems):
    parts = [(cells_hbm, cells, 0), (cells_hbm, cells, 1), (fh_hbm, fh, 0), (fl_hbm, fl, 0), (fh_hbm, fh, 1), (fl_hbm, fl, 1), (fh_hbm, fh, 2), (fl_hbm, fl, 2)]
    copies = []
    for n, (src, dst, block) in enumerate(parts):
        rows = pl.ds(block * 256, 256)
        copies.append(pltpu.make_async_copy(src.at[rows], dst.at[rows], sems.at[n]))
        copies[n].start()

    def prepare(n):
        for r in range(0, 256, 32):
            b0, b1, b2 = [cells[n * 256 + r : n * 256 + r + 32, m * THIRD : (m + 1) * THIRD] for m in range(3)]
            both = b1 + b2
            for at, value in enumerate((b0 + both, b0 - 0.5 * both, ROOT3 * (b1 - b2))):
                half[n, at, r : r + 32, :], wide[n, at, r : r + 32, :] = split(value)

    def store(freqs, p, n):
        for par in range(2):
            for c in range(2):
                out_ref[pl.ds(p * 8 + (2 * n + c) * 2 + par, 128, stride=24), :] = freqs[par][:, c * 128 : (c + 1) * 128]

    def transform(p, n):
        basis = (fh[p * 256 : (p + 1) * 256, :], fl[p * 256 : (p + 1) * 256, :])

        def one(at):
            return dot3(basis, (half[n, at], wide[n, at]), NT)

        if p == 0:
            whole = one(0)
            store((whole[0:128], whole[128:]), p, n)
        else:
            real, imag = one(1), one(2)
            if p == 1:
                store((real[0:128] - imag[128:], real[128:] + imag[0:128]), p, n)
            else:
                store((real[0:128] + imag[128:], real[128:] - imag[0:128]), p, n)

    for copy in copies[0:1]:
        copy.wait()
    prepare(0)
    for copy in copies[1:2]:
        copy.wait()
    prepare(1)
    for copy in copies[2:]:
        copy.wait()
    transform(1, 0)
    transform(1, 1)
    transform(2, 0)
    transform(2, 1)
    transform(0, 0)
    transform(0, 1)


def inverse_z_kernel(in_ref, fh_ref, fl_ref, out_hbm, out, sems):
    base_f = (fh_ref[0:256, :], fl_ref[0:256, :])
    pair_f = (fh_ref[256:, :], fl_ref[256:, :])
    copies = []
    for n in range(2):

        def columns(*ks):
            blocks = []
            for c in (2 * n, 2 * n + 1):
                got = [in_ref[pl.ds(abs(k) // 2 * 8 + c * 2 + abs(k) % 2, 128, stride=24), :].T for k in ks]
                blocks.append(jnp.concatenate(got, axis=1))
            return split(jnp.concatenate(blocks, axis=0))

        base = dot3(columns(0, 1), base_f)
        hi, lo = columns(2, 3, 4, 5)
        real = dot3((hi, lo), pair_f)

        def turned(x):
            y2, y3, y4, y5 = [x[:, at * 128 : (at + 1) * 128] for at in range(4)]
            return jnp.concatenate([y3, -y2, -y5, y4], axis=1)

        imag = ROOT3 * dot3((turned(hi), turned(lo)), pair_f)
        low = base - 0.5 * real
        for q in range(2):
            rows = slice(q * 128, (q + 1) * 128)
            at = n * 256 + q * 128
            out[at : at + 128, 0:THIRD] = base[rows] + real[rows]
            out[at : at + 128, THIRD : 2 * THIRD] = low[rows] + imag[rows]
            out[at : at + 128, 2 * THIRD :] = low[rows] - imag[rows]
            here = pl.ds(at, 128)
            copies.append(pltpu.make_async_copy(out.at[here], out_hbm.at[here], sems.at[2 * n + q]))
            copies[-1].start()
    for copy in copies:
        copy.wait()


def forward_xy_kernel(
    dev_ref, in_ref, taps_ref, tabh_ref, tabl_ref, qxh_ref, qxl_ref, qyh_ref, qyl_ref, spec_hbm, stat_hbm, fh_ref, fl_ref,
    lo_ref, hi_ref, weight_ref, spec_ref, pad_ref, lam_ref, zlam_ref, stat_ref, sems,
):
    taps, rows, cols, lam_x, lam_y = plane_response(taps_ref, pad_ref, (tabh_ref[...], tabl_ref[...]))
    lam_ref[...] = lam_x[0:128] * lam_y
    lam_edge = lam_x[128:129] * lam_y
    zlam = jnp.broadcast_to(depth_response(dev_ref[0], taps[2:3, :])[2], (8, NY))
    for slot, k in enumerate((0, 1, 2, 4)):
        zlam_ref[slot * 8 : slot * 8 + 8, :] = jnp.broadcast_to(zlam[k : k + 1, :], (8, NY))
    left, right = (qxh_ref[...], qxl_ref[...]), (qyh_ref[...], qyl_ref[...])

    def gather(p):
        for i in range(16):
            for high in range(2):
                first = [(i * 8 + high * 4 + j) * 24 + p * 8 for j in range(4)]
                got = swap_blocks([in_ref[at : at + 8, :] for at in first])
                for r in (0, 2):
                    at = slice((i * 4 + r) * 8, (i * 4 + r + 2) * 8)
                    lanes = slice(high * 128, (high + 1) * 128)
                    fh_ref[p, at, lanes], fl_ref[p, at, lanes] = split(jnp.concatenate(got[r : r + 2], axis=0))

    def along_y(p):
        for h in range(2):
            at = slice(h * 256, (h + 1) * 256)
            field = dot3((fh_ref[p, at], fl_ref[p, at]), right)
            at = slice(p * 512 + h * 256, p * 512 + (h + 1) * 256)
            lo_ref[at, :], hi_ref[at, :] = field[:, :128], field[:, 128:]

    top = lax.broadcasted_iota(jnp.int32, (8, NY), 0) == 0
    edges = []
    plain = [jnp.zeros((8, NY), F32)] * 3

    def along_x(p):
        specs = []
        for par in range(2):
            plane = [ref[pl.ds(p * 512 + par, 256, stride=2), :] for ref in (lo_ref, hi_ref)]
            specs.append(dot3(left, split(jnp.concatenate(plane, axis=1))))
        weights = []
        for par, spec in enumerate(specs):
            spec_ref[2 * p + par] = spec
            upper, lower = spec[0:128], spec[128:256]
            upper, lower = upper * upper, lower * lower
            edges.append(lower[0:1, :])
            weights.append(jnp.concatenate([upper[0:8] + jnp.where(top, 0.0, lower[0:8]), upper[8:] + lower[8:]], axis=0))
        for slot, weight in enumerate(weights if p == 0 else [weights[0] + weights[1]], 0 if p == 0 else p + 1):
            weight_ref[slot] = weight
            w = weight.reshape(16, 8, NY)
            l = lam_ref[...].reshape(16, 8, NY) * zlam_ref[slot * 8 : slot * 8 + 8, :]
            for n, value in enumerate((w, w * l, w * l * l)):
                plain[n] = plain[n] + value.sum(axis=0)

    gather(0)
    along_y(0)
    gather(1)
    along_y(1)
    gather(2)
    along_x(0)
    along_y(2)
    along_x(1)
    along_x(2)
    copies = [pltpu.make_async_copy(spec_ref, spec_hbm, sems.at[0])]
    copies[0].start()

    row = lax.broadcasted_iota(jnp.int32, (8, NY), 0)
    edge = jnp.zeros((8, NY), F32)
    for slot, value in enumerate((edges[0], edges[1], edges[2] + edges[3], edges[4] + edges[5])):
        edge = jnp.where(row == slot, value, edge)
    zedge = jnp.where(row < 2, zlam, jnp.where(row == 2, zlam_ref[16:24, :], zlam_ref[24:32, :]))
    edge_lam = lam_edge * zedge

    def sums(*funcs):
        def more(parts, w, l):
            w, l = w.reshape(-1, 8, NY), l.reshape(-1, 8, NY)
            return [part + func(w, l).sum(axis=0) for part, func in zip(parts, funcs)]

        def plane(slot, parts):
            zlam = jnp.concatenate([zlam_ref[pl.ds(pl.multiple_of(slot * 8, 8), 8), :]] * 4, axis=0)
            for r in range(4):
                parts = more(parts, weight_ref[slot, r * 32 : (r + 1) * 32, :], lam_ref[r * 32 : (r + 1) * 32, :] * zlam)
            return parts

        parts = more([jnp.zeros((8, NY), F32) for _ in funcs], edge, edge_lam)
        return [total(p) for p in lax.fori_loop(0, 4, plane, parts)]

    first = edge * edge_lam
    zero, one, two = [total(p) for p in (plain[0] + edge, plain[1] + first, plain[2] + first * edge_lam)]
    mean = one / jnp.maximum(zero, TINY)
    tau = two / jnp.maximum(one, TINY)

    def centred(w, l):
        d = l - mean
        return w * d * d

    def tilted(w, l):
        d = l - tau
        return w * l * d * d

    var, tilt = sums(centred, tilted)
    step = tau - mean
    slope = (tilt + one * step * step) / jnp.maximum(var, TINY)
    ratio = var / jnp.maximum(zero, TINY)

    def second(w, l):
        d = (l - slope) * (l - mean) - ratio
        return w * d * d

    (last,) = sums(second)
    lane = lax.broadcasted_iota(jnp.int32, (8, 128), 1)
    packed = jnp.zeros((8, 128), F32)
    for n, value in enumerate((zero, mean, tau, var, slope, ratio, tilt, last, one)):
        packed = jnp.where(lane == n, value[:, 0:128], packed)
    for n in range(16):
        stat_ref[n * 8 : n * 8 + 8, :] = packed
    copies.append(pltpu.make_async_copy(stat_ref, stat_hbm, sems.at[1]))
    copies[1].start()
    for copy in copies:
        copy.wait()


def inverse_xy_kernel(
    dev_ref, spec_hbm, taps_hbm, tabh_hbm, tabl_hbm, qxh_hbm, qxl_hbm, qyh_hbm, qyl_hbm, out_ref, ulo_ref, uhi_ref, vlo_ref,
    vhi_ref, spec_ref, taps_ref, tabh_ref, tabl_ref, qxh_ref, qxl_ref, qyh_ref, qyl_ref, pad_ref, lam_ref, zed_ref, sems,
):
    pairs = [(taps_hbm, taps_ref), (tabh_hbm, tabh_ref), (tabl_hbm, tabl_ref), (qxh_hbm, qxh_ref), (qxl_hbm, qxl_ref)]
    pairs += [(qyh_hbm, qyh_ref), (qyl_hbm, qyl_ref), (spec_hbm, spec_ref)]
    copies = [pltpu.make_async_copy(src, dst, sems.at[n]) for n, (src, dst) in enumerate(pairs)]
    for copy in copies:
        copy.start()
    for copy in copies[:7]:
        copy.wait()
    taps, rows, cols, lam_x, lam_y = plane_response(taps_ref, pad_ref, (tabh_ref[...], tabl_ref[...]))
    lam_ref[...] = lam_x * lam_y
    for n, value in enumerate(depth_response(dev_ref[0], taps[2:3, :])):
        zed_ref[n * 8 : n * 8 + 8, :] = jnp.broadcast_to(value, (8, NY))
    qt = (qxh_ref[...].astype(F32) + qxl_ref[...].astype(F32)).T
    turned = jnp.concatenate([-qt[:, 128:], qt[:, :128]], axis=1)
    left = split(qt * rows[0:1, 0:NX] + turned * rows[0:1, NX:])
    q = (qyh_ref[...].astype(F32) + qyl_ref[...].astype(F32)).T
    turned = jnp.concatenate([-q[128:, :], q[:128, :]], axis=0)
    right = split(q * cols[0:NY, 1:2] + turned * cols[NY:, 1:2])
    copies[7].wait()
    refs = (ulo_ref, uhi_ref, vlo_ref, vhi_ref)
    for p in range(3):
        e, o = 2 * p, 2 * p + 1
        a, b = spec_ref[e], spec_ref[o]
        lam = lam_ref[...]
        la, lb = a * (lam * zed_ref[16 + e : 17 + e, :]), b * (lam * zed_ref[16 + o : 17 + o, :])
        for k, x, y, lx, ly in ((e, a, b, la, lb), (o, b, a, lb, la)):
            re, im = zed_ref[k : k + 1, :], zed_ref[8 + k : 9 + k, :]
            both = jnp.concatenate([re * x + im * y, re * lx + im * ly], axis=1)
            back = dot3(left, split(both))
            for n, ref in enumerate(refs):
                ref[pl.ds(p * 512 + k % 2, 256, stride=2), :] = back[:, n * 128 : (n + 1) * 128]

        for which, pair in enumerate((refs[0:2], refs[2:4])):
            field = jnp.concatenate([ref[p * 512 : (p + 1) * 512, :] for ref in pair], axis=1)
            field = dot3(split(field), right)
            for i in range(16):
                for high in range(2):
                    got = [field[(i * 4 + r) * 8 : (i * 4 + r + 1) * 8, high * 128 : (high + 1) * 128] for r in range(4)]
                    for j, piece in enumerate(swap_blocks(got)):
                        at = (i * 8 + high * 4 + j) * 24 + p * 8
                        out_ref[which, at : at + 8, :] = piece


def weights_of(stats_ref):
    zero, mean, tau, var, slope, ratio, tilt, last, one = [
        jnp.broadcast_to(stats_ref[n : n + 1, :], (8, 128)) for n in range(9)
    ]
    add = lane_total

    all_zero = add(zero)
    all_mean = add(one) / all_zero
    shift = mean - all_mean
    all_var = add(var + shift * shift * zero)
    all_ratio = all_var / all_zero
    lean = tau - all_mean
    all_slope = add(tilt + one * lean * lean) / all_var
    lean = tau - all_mean - all_var / (all_zero * all_mean)
    all_tilt = add(tilt + one * lean * lean)
    first = shift + (slope - all_slope)
    const = shift * (mean - all_slope) + ratio - all_ratio
    all_last = add(last + first * first * var + const * const * zero)

    scale = 1.0 / all_mean
    b2, a2, b3 = all_ratio * (scale * scale), all_tilt / all_var * scale, all_last / all_tilt * scale

    def entries(square):
        entry_a, entry_b = 1.0 + b2 + square, a2 + b3 + square
        rest = b2 * (b3 + square) + square * entry_b
        return entry_a, entry_b, rest, entry_b + rest

    lane = lax.broadcasted_iota(jnp.int32, (8, 128), 1)
    log_grid = (jnp.minimum(lane, 15).astype(F32) * 0.2 - 3.0) * float(np.log(10.0))
    square = jnp.exp(2.0 * log_grid)
    entry_a, entry_b, rest, determ = entries(square)
    inverse = 1.0 / (determ + square * (entry_a + entry_b))
    miss = rest * inverse
    other = b3 + square
    scores = 3.0 * (miss * miss + (b2 * inverse) * ((other * other + a2 * b3) * inverse))
    shifted = scores + 0.05
    shifted = shifted * shifted
    weights = jnp.where(lane < 16, 1.0 / (shifted * shifted), 0.0)
    chosen = jnp.exp(2.0 * (add(weights * log_grid) / add(weights)))
    entry_a, entry_b, rest, determ = entries(chosen)
    c1 = scale / determ
    return c1 * (1.0 + b2 + entry_b), -c1 * scale


def combine_kernel(stat_ref, both_ref, out_ref, rows_ref):
    rows_ref[...] = stat_ref[...].T[0:16]
    c1, c2 = weights_of(rows_ref)

    def rows(n, carry):
        for t in range(24):
            at = pl.ds(pl.multiple_of(n * 192 + t * 8, 8), 8)
            out_ref[at, :] = c1 * both_ref[0, at, :] + c2 * both_ref[1, at, :]
        return carry

    lax.fori_loop(0, 16, rows, 0)


def make_local():
    vmem = pl.BlockSpec(memory_space=pltpu.VMEM)
    smem = pl.BlockSpec(memory_space=pltpu.SMEM)
    hbm = pl.BlockSpec(memory_space=pltpu.HBM)
    params = pltpu.CompilerParams(vmem_limit_bytes=40 << 20)

    depth = halves(depth_basis())
    basis = plane_basis(NX)
    place = np.arange(NX)
    qx = halves(basis[:, 16 * (place // 16) + 4 * (place % 4) + (place // 4) % 4])
    qy = halves(basis.T)
    table = halves(plane_table(NX))
    half_rows = pltpu.VMEM((1536, 128), F32)
    tile = pltpu.VMEM((8, 128), F32)
    planes = pltpu.VMEM((6, NX, NY), F32)

    def exchange(chunks):
        return lax.all_to_all(chunks, ("gx", "gy"), 0, 0, tiled=True)

    def in_hbm(*arrays):
        return [pltpu.with_memory_space_constraint(jnp.asarray(x), pltpu.HBM) for x in arrays]

    def local(observed, psf_taps):
        dev = (lax.axis_index("gx") * 8 + lax.axis_index("gy")).astype(jnp.int32).reshape(1)
        sent = pl.pallas_call(
            forward_z_kernel,
            in_specs=[smem] + [hbm] * 3,
            out_specs=vmem,
            out_shape=pltpu.VMEM((3072, 128), F32),
            scratch_shapes=[pltpu.VMEM((512, NZ), F32)]
            + [pltpu.VMEM((3 * THIRD, THIRD), BF16)] * 2
            + [pltpu.VMEM((2, 3, 256, THIRD), BF16)] * 2
            + [pltpu.SemaphoreType.DMA((8,))],
            compiler_params=params,
            name="forward_z",
        )(dev, *in_hbm(observed.reshape(512, NZ), *depth))
        got = exchange(sent.reshape(128, 24, 128)).reshape(3072, 128)
        spec, stat = pl.pallas_call(
            forward_xy_kernel,
            in_specs=[smem] + [vmem] * 8,
            out_specs=[hbm] * 2,
            out_shape=[pltpu.HBM((6, NX, NY), F32), pltpu.HBM((128, 128), F32)],
            scratch_shapes=[pltpu.VMEM((3, 512, NY), BF16)] * 2
            + [half_rows] * 2
            + [pltpu.VMEM((4, 128, NY), F32), planes, tile, pltpu.VMEM((128, NY), F32), pltpu.VMEM((32, NY), F32)]
            + [pltpu.VMEM((128, 128), F32), pltpu.SemaphoreType.DMA((2,))],
            compiler_params=params,
            name="forward_xy",
        )(dev, got, psf_taps, *table, *qx, *qy)
        stats = exchange(stat.reshape(128, 1, 128)).reshape(128, 128)
        both = pl.pallas_call(
            inverse_xy_kernel,
            in_specs=[smem] + [hbm] * 8,
            out_specs=vmem,
            out_shape=pltpu.VMEM((2, 3072, 128), F32),
            scratch_shapes=[half_rows] * 4
            + [planes, pltpu.VMEM((3, TAPS), F32)]
            + [pltpu.VMEM((32, 2 * NX), BF16)] * 2
            + [pltpu.VMEM((NX, NX), BF16)] * 4
            + [tile, pltpu.VMEM((NX, NY), F32), pltpu.VMEM((24, NY), F32)]
            + [pltpu.SemaphoreType.DMA((8,))],
            compiler_params=params,
            name="inverse_xy",
        )(dev, *in_hbm(spec, psf_taps, *table, *qx, *qy))
        sent = pl.pallas_call(
            combine_kernel,
            in_specs=[vmem] * 2,
            out_specs=vmem,
            out_shape=pltpu.VMEM((3072, 128), F32),
            scratch_shapes=[pltpu.VMEM((16, 128), F32)],
            compiler_params=params,
            name="combine",
        )(stats, both)
        got = exchange(sent.reshape(128, 24, 128)).reshape(3072, 128)
        out = pl.pallas_call(
            inverse_z_kernel,
            in_specs=[vmem] * 3,
            out_specs=hbm,
            out_shape=jax.ShapeDtypeStruct((512, NZ), F32),
            scratch_shapes=[pltpu.VMEM((512, NZ), F32), pltpu.SemaphoreType.DMA((4,))],
            compiler_params=params,
            name="inverse_z",
        )(got, *depth)
        return out.reshape(16, 32, NZ)

    return local


def solution(mesh):
    in_specs = (P("gx", "gy", None), P())
    out_specs = P("gx", "gy", None)
    return jax.shard_map(make_local(), mesh=mesh, in_specs=in_specs, out_specs=out_specs, check_vma=False)
```

```python
import jax
import jax.numpy as jnp
import numpy as np
from jax import lax
from jax.experimental import pallas as pl
from jax.experimental.pallas import tpu as pltpu
from jax.sharding import PartitionSpec as P

NX, NY, NZ, TAPS = 256, 256, 768, 31
HALF = TAPS // 2
THIRD = NZ // 3
ROOT3 = float(np.sqrt(3.0) / 2.0)
F32, BF16 = jnp.float32, jnp.bfloat16
TINY = 1e-30
NN = ((1,), (0,))
NT = ((1,), (1,))


def halves(values):
    hi = np.asarray(values, np.float32).astype(BF16)
    lo = (values - hi.astype(np.float64)).astype(np.float32).astype(BF16)
    return hi, lo


def plane_basis(n):
    pos = np.arange(n)
    freq = np.arange(n // 2)[:, None]
    angle = 2.0 * np.pi * ((freq * pos) % n) / n
    basis = np.concatenate([np.cos(angle), np.sin(angle)]) * np.sqrt(2.0 / n)
    basis[0] = 1.0 / np.sqrt(n)
    basis[n // 2] = np.where(pos % 2 == 0, 1.0, -1.0) / np.sqrt(n)
    return basis


def plane_table(n):
    freq = np.arange(n) % (n // 2)
    freq[n // 2] = n // 2
    turn = ((np.arange(TAPS) - HALF)[:, None] * freq) % n
    table = np.zeros((32, 2 * n))
    table[:TAPS, :n] = np.cos(2.0 * np.pi * turn / n)
    table[:TAPS, n:] = np.where(turn % (n // 2) == 0, 0.0, np.sin(2.0 * np.pi * turn / n))
    return table


def depth_basis():
    pos = np.arange(THIRD)
    dev = np.arange(128)[:, None]

    def blocks(freq):
        angle = 2.0 * np.pi * ((freq * pos) % NZ) / NZ
        return np.sqrt(2.0 / NZ) * np.cos(angle), np.sqrt(2.0 / NZ) * np.sin(angle)

    cos, sin = blocks(3 * dev)
    cos[0] = 1.0 / np.sqrt(NZ)
    sin[0] = np.where(pos % 2 == 0, 1.0, -1.0) / np.sqrt(NZ)
    cos_one, sin_one = blocks(np.concatenate([3 * dev + 1, -(3 * dev + 2)]))
    return np.concatenate([cos, sin, cos_one, sin_one - cos_one, sin_one + cos_one])


def split(values):
    hi = values.astype(BF16)
    return hi, (values - hi.astype(F32)).astype(BF16)


def dot3(left, right, dims=NN):
    def one(a, b):
        return lax.dot_general(a, b, (dims, ((), ())), preferred_element_type=F32)

    return one(left[0], right[0]) + (one(left[0], right[1]) + one(left[1], right[0]))


def lane_total(values):
    return jnp.broadcast_to(jnp.sum(values, axis=1, keepdims=True), (8, 128))


def total(values):
    sums = lane_total(values[:, :128] + values[:, 128:])
    sums = jnp.broadcast_to(jnp.sum(sums, axis=0, keepdims=True), (8, 128))
    return jnp.concatenate([sums, sums], axis=1)


def depth_response(dev, taps):
    row = lax.broadcasted_iota(jnp.int32, (8, 128), 0)
    offset = lax.broadcasted_iota(jnp.int32, (8, 128), 1).astype(F32) - float(HALF)
    pair = dev * 3 + row // 2
    odd = row % 2
    first = pair == 0
    freq = jnp.where(first & (odd == 1), NZ // 2, pair).astype(F32)
    turn = freq * offset
    turn = turn - float(NZ) * jnp.floor(turn * (1.0 / NZ))
    angle = turn * (2.0 * np.pi / NZ)
    real = jnp.sum(jnp.cos(angle) * taps, axis=1, keepdims=True)
    imag = jnp.sum(jnp.where(first, 0.0, jnp.sin(angle)) * taps, axis=1, keepdims=True)
    return real, jnp.where(odd[:, 0:1] == 1, -imag, imag), real * real + imag * imag


def swap_blocks(vecs):
    block = lax.broadcasted_iota(jnp.int32, vecs[0].shape, 1) // 32
    odd, high = (block & 1) != 0, (block & 2) != 0

    def pick(arrays, first):
        pairs = [jnp.where(odd, arrays[(n + 1) % 4], arrays[n]) for n in range(4)]
        return [jnp.where(high, pairs[(n + 2) % 4], pairs[n % 4]) for n in first]

    turned = [pltpu.roll(v, 32 * n, 1) if n else v for n, v in enumerate(pick(vecs, range(4)))]
    return pick(turned, (0, 3, 2, 1))


def plane_response(taps_ref, pad_ref, table):
    pad_ref[...] = jnp.zeros((8, 128), F32)
    pad_ref[0:3, 0:TAPS] = taps_ref[...]
    taps = pad_ref[...]
    rows = dot3(split(taps[:, 0:32]), table)
    cols = rows.T
    lam_x = cols[0:NX, 0:1] * cols[0:NX, 0:1] + cols[NX:, 0:1] * cols[NX:, 0:1]
    lam_y = rows[1:2, 0:NY] * rows[1:2, 0:NY] + rows[1:2, NY:] * rows[1:2, NY:]
    return taps, rows, cols, lam_x, lam_y


def forward_z_kernel(dev_ref, cells_hbm, fh_hbm, fl_hbm, out_ref, cells, fh, fl, half, wide, sems):
    parts = [(cells_hbm, cells, 0, 256), (fh_hbm, fh, 0, 1024), (fl_hbm, fl, 0, 1024), (cells_hbm, cells, 1, 256)]
    copies = []
    for n, (src, dst, block, size) in enumerate(parts):
        rows = pl.ds(block * 256, size)
        copies.append(pltpu.make_async_copy(src.at[rows], dst.at[rows], sems.at[n]))
        copies[n].start()

    def prepare(n):
        for r in range(0, 256, 32):
            b0, b1, b2 = [cells[n * 256 + r : n * 256 + r + 32, m * THIRD : (m + 1) * THIRD] for m in range(3)]
            both = b1 + b2
            p, q = b0 - 0.5 * both, ROOT3 * (b1 - b2)
            for at, value in enumerate((b0 + both, p + q, p, q)):
                half[n, at, r : r + 32, :], wide[n, at, r : r + 32, :] = split(value)

    def store(freqs, p, n):
        for par in range(2):
            for c in range(2):
                out_ref[pl.ds(p * 8 + (2 * n + c) * 2 + par, 128, stride=24), :] = freqs[par][:, c * 128 : (c + 1) * 128]

    def product(block, n):
        rows = slice(block * 256, (block + 1) * 256)
        return dot3((fh[rows, :], fl[rows, :]), (half[n, block], wide[n, block]), NT)


    def transform(n):
        one, two, three = product(1, n), product(2, n), product(3, n)
        real, imag = one - three, one + two
        store((real[0:128], imag[0:128]), 1, n)
        store((real[128:], -imag[128:]), 2, n)
        whole = product(0, n)
        store((whole[0:128], whole[128:]), 0, n)

    copies[0].wait()
    prepare(0)
    copies[1].wait()
    copies[2].wait()
    transform(0)
    copies[3].wait()
    prepare(1)
    transform(1)


def inverse_z_kernel(in_ref, fh_ref, fl_ref, out_hbm, out, sems):
    copies = []

    def product(values, block):
        rows = slice(block * 256, (block + 1) * 256)
        return dot3(split(values), (fh_ref[rows, :], fl_ref[rows, :]))

    for n in range(2):

        def columns(*ks):
            blocks = []
            for c in (2 * n, 2 * n + 1):
                got = [in_ref[pl.ds(k // 2 * 8 + c * 2 + k % 2, 128, stride=24), :].T for k in ks]
                blocks.append(jnp.concatenate(got, axis=1))
            return jnp.concatenate(blocks, axis=0)

        real, imag = columns(2, 4), columns(3, 5)
        imag = jnp.concatenate([imag[:, :128], -imag[:, 128:]], axis=1)
        one, two, three = product(real + imag, 1), product(imag, 2), product(real, 3)
        base = product(columns(0, 1), 0)
        p, q = one + two, ROOT3 * (one - three)
        low = base - 0.5 * p
        for half in range(2):
            rows = slice(half * 128, (half + 1) * 128)
            at = n * 256 + half * 128
            out[at : at + 128, 0:THIRD] = base[rows] + p[rows]
            out[at : at + 128, THIRD : 2 * THIRD] = low[rows] + q[rows]
            out[at : at + 128, 2 * THIRD :] = low[rows] - q[rows]
            here = pl.ds(at, 128)
            copies.append(pltpu.make_async_copy(out.at[here], out_hbm.at[here], sems.at[2 * n + half]))
            copies[-1].start()
    for copy in copies:
        copy.wait()


def forward_xy_kernel(
    dev_ref, in_ref, taps_ref, tabh_ref, tabl_ref, qxh_ref, qxl_ref, qyh_ref, qyl_ref, spec_hbm, stat_hbm, fh_ref, fl_ref,
    lo_ref, hi_ref, weight_ref, spec_ref, pad_ref, lam_ref, zlam_ref, stat_ref, sems,
):
    taps, rows, cols, lam_x, lam_y = plane_response(taps_ref, pad_ref, (tabh_ref[...], tabl_ref[...]))
    lam_ref[...] = lam_x[0:128] * lam_y
    lam_edge = lam_x[128:129] * lam_y
    zlam = jnp.broadcast_to(depth_response(dev_ref[0], taps[2:3, :])[2], (8, NY))
    for slot, k in enumerate((0, 1, 2, 4)):
        zlam_ref[slot * 8 : slot * 8 + 8, :] = jnp.broadcast_to(zlam[k : k + 1, :], (8, NY))
    left, right = (qxh_ref[...], qxl_ref[...]), (qyh_ref[...], qyl_ref[...])

    def gather(p):
        for i in range(16):
            for high in range(2):
                first = [(i * 8 + high * 4 + j) * 24 + p * 8 for j in range(4)]
                got = swap_blocks([in_ref[at : at + 8, :] for at in first])
                for r in (0, 2):
                    at = slice((i * 4 + r) * 8, (i * 4 + r + 2) * 8)
                    lanes = slice(high * 128, (high + 1) * 128)
                    fh_ref[p, at, lanes], fl_ref[p, at, lanes] = split(jnp.concatenate(got[r : r + 2], axis=0))

    def along_y(p):
        for h in range(2):
            at = slice(h * 256, (h + 1) * 256)
            field = dot3((fh_ref[p, at], fl_ref[p, at]), right)
            at = slice(p * 512 + h * 256, p * 512 + (h + 1) * 256)
            lo_ref[at, :], hi_ref[at, :] = field[:, :128], field[:, 128:]

    top = lax.broadcasted_iota(jnp.int32, (8, NY), 0) == 0
    edges = []
    plain = [jnp.zeros((8, NY), F32)] * 3

    def along_x(p):
        specs = []
        for par in range(2):
            plane = [ref[pl.ds(p * 512 + par, 256, stride=2), :] for ref in (lo_ref, hi_ref)]
            specs.append(dot3(left, split(jnp.concatenate(plane, axis=1))))
        weights = []
        for par, spec in enumerate(specs):
            spec_ref[2 * p + par] = spec
            upper, lower = spec[0:128], spec[128:256]
            upper, lower = upper * upper, lower * lower
            edges.append(lower[0:1, :])
            weights.append(jnp.concatenate([upper[0:8] + jnp.where(top, 0.0, lower[0:8]), upper[8:] + lower[8:]], axis=0))
        for slot, weight in enumerate(weights if p == 0 else [weights[0] + weights[1]], 0 if p == 0 else p + 1):
            weight_ref[slot] = weight
            w = weight.reshape(16, 8, NY)
            l = lam_ref[...].reshape(16, 8, NY) * zlam_ref[slot * 8 : slot * 8 + 8, :]
            for n, value in enumerate((w, w * l, w * l * l)):
                plain[n] = plain[n] + value.sum(axis=0)

    gather(0)
    along_y(0)
    gather(1)
    along_y(1)
    gather(2)
    along_x(0)
    along_y(2)
    along_x(1)
    along_x(2)
    copies = [pltpu.make_async_copy(spec_ref, spec_hbm, sems.at[0])]
    copies[0].start()

    row = lax.broadcasted_iota(jnp.int32, (8, NY), 0)
    edge = jnp.zeros((8, NY), F32)
    for slot, value in enumerate((edges[0], edges[1], edges[2] + edges[3], edges[4] + edges[5])):
        edge = jnp.where(row == slot, value, edge)
    zedge = jnp.where(row < 2, zlam, jnp.where(row == 2, zlam_ref[16:24, :], zlam_ref[24:32, :]))
    edge_lam = lam_edge * zedge

    def sums(*funcs):
        def more(parts, w, l):
            w, l = w.reshape(-1, 8, NY), l.reshape(-1, 8, NY)
            return [part + func(w, l).sum(axis=0) for part, func in zip(parts, funcs)]

        def plane(slot, parts):
            zlam = jnp.concatenate([zlam_ref[pl.ds(pl.multiple_of(slot * 8, 8), 8), :]] * 4, axis=0)
            for r in range(4):
                parts = more(parts, weight_ref[slot, r * 32 : (r + 1) * 32, :], lam_ref[r * 32 : (r + 1) * 32, :] * zlam)
            return parts

        parts = more([jnp.zeros((8, NY), F32) for _ in funcs], edge, edge_lam)
        return [total(p) for p in lax.fori_loop(0, 4, plane, parts)]

    first = edge * edge_lam
    zero, one, two = [total(p) for p in (plain[0] + edge, plain[1] + first, plain[2] + first * edge_lam)]
    mean = one / jnp.maximum(zero, TINY)
    tau = two / jnp.maximum(one, TINY)

    def centred(w, l):
        d = l - mean
        return w * d * d

    def tilted(w, l):
        d = l - tau
        return w * l * d * d

    var, tilt = sums(centred, tilted)
    step = tau - mean
    slope = (tilt + one * step * step) / jnp.maximum(var, TINY)
    ratio = var / jnp.maximum(zero, TINY)

    def second(w, l):
        d = (l - slope) * (l - mean) - ratio
        return w * d * d

    (last,) = sums(second)
    lane = lax.broadcasted_iota(jnp.int32, (8, 128), 1)
    packed = jnp.zeros((8, 128), F32)
    for n, value in enumerate((zero, mean, tau, var, slope, ratio, tilt, last, one)):
        packed = jnp.where(lane == n, value[:, 0:128], packed)
    for n in range(16):
        stat_ref[n * 8 : n * 8 + 8, :] = packed
    copies.append(pltpu.make_async_copy(stat_ref, stat_hbm, sems.at[1]))
    copies[1].start()
    for copy in copies:
        copy.wait()


def inverse_xy_kernel(
    dev_ref, spec_hbm, taps_hbm, tabh_hbm, tabl_hbm, qxh_hbm, qxl_hbm, qyh_hbm, qyl_hbm, out_ref, ulo_ref, uhi_ref, vlo_ref,
    vhi_ref, spec_ref, taps_ref, tabh_ref, tabl_ref, qxh_ref, qxl_ref, qyh_ref, qyl_ref, pad_ref, lam_ref, zed_ref, sems,
):
    pairs = [(taps_hbm, taps_ref), (tabh_hbm, tabh_ref), (tabl_hbm, tabl_ref), (qxh_hbm, qxh_ref), (qxl_hbm, qxl_ref)]
    pairs += [(qyh_hbm, qyh_ref), (qyl_hbm, qyl_ref), (spec_hbm, spec_ref)]
    copies = [pltpu.make_async_copy(src, dst, sems.at[n]) for n, (src, dst) in enumerate(pairs)]
    for copy in copies:
        copy.start()
    for copy in copies[:7]:
        copy.wait()
    taps, rows, cols, lam_x, lam_y = plane_response(taps_ref, pad_ref, (tabh_ref[...], tabl_ref[...]))
    lam_ref[...] = lam_x * lam_y
    for n, value in enumerate(depth_response(dev_ref[0], taps[2:3, :])):
        zed_ref[n * 8 : n * 8 + 8, :] = jnp.broadcast_to(value, (8, NY))
    qt = (qxh_ref[...].astype(F32) + qxl_ref[...].astype(F32)).T
    turned = jnp.concatenate([-qt[:, 128:], qt[:, :128]], axis=1)
    left = split(qt * rows[0:1, 0:NX] + turned * rows[0:1, NX:])
    q = (qyh_ref[...].astype(F32) + qyl_ref[...].astype(F32)).T
    turned = jnp.concatenate([-q[128:, :], q[:128, :]], axis=0)
    right = split(q * cols[0:NY, 1:2] + turned * cols[NY:, 1:2])
    copies[7].wait()
    refs = (ulo_ref, uhi_ref, vlo_ref, vhi_ref)
    for p in range(3):
        e, o = 2 * p, 2 * p + 1
        a, b = spec_ref[e], spec_ref[o]
        lam = lam_ref[...]
        la, lb = a * (lam * zed_ref[16 + e : 17 + e, :]), b * (lam * zed_ref[16 + o : 17 + o, :])
        for k, x, y, lx, ly in ((e, a, b, la, lb), (o, b, a, lb, la)):
            re, im = zed_ref[k : k + 1, :], zed_ref[8 + k : 9 + k, :]
            both = jnp.concatenate([re * x + im * y, re * lx + im * ly], axis=1)
            back = dot3(left, split(both))
            for n, ref in enumerate(refs):
                ref[pl.ds(p * 512 + k % 2, 256, stride=2), :] = back[:, n * 128 : (n + 1) * 128]

        for which, pair in enumerate((refs[0:2], refs[2:4])):
            field = jnp.concatenate([ref[p * 512 : (p + 1) * 512, :] for ref in pair], axis=1)
            field = dot3(split(field), right)
            for i in range(16):
                for high in range(2):
                    got = [field[(i * 4 + r) * 8 : (i * 4 + r + 1) * 8, high * 128 : (high + 1) * 128] for r in range(4)]
                    for j, piece in enumerate(swap_blocks(got)):
                        at = (i * 8 + high * 4 + j) * 24 + p * 8
                        out_ref[which, at : at + 8, :] = piece


def weights_of(stats_ref):
    zero, mean, tau, var, slope, ratio, tilt, last, one = [
        jnp.broadcast_to(stats_ref[n : n + 1, :], (8, 128)) for n in range(9)
    ]
    add = lane_total

    all_zero = add(zero)
    all_mean = add(one) / all_zero
    shift = mean - all_mean
    all_var = add(var + shift * shift * zero)
    all_ratio = all_var / all_zero
    lean = tau - all_mean
    all_slope = add(tilt + one * lean * lean) / all_var
    lean = tau - all_mean - all_var / (all_zero * all_mean)
    all_tilt = add(tilt + one * lean * lean)
    first = shift + (slope - all_slope)
    const = shift * (mean - all_slope) + ratio - all_ratio
    all_last = add(last + first * first * var + const * const * zero)

    scale = 1.0 / all_mean
    b2, a2, b3 = all_ratio * (scale * scale), all_tilt / all_var * scale, all_last / all_tilt * scale

    def entries(square):
        entry_a, entry_b = 1.0 + b2 + square, a2 + b3 + square
        rest = b2 * (b3 + square) + square * entry_b
        return entry_a, entry_b, rest, entry_b + rest

    lane = lax.broadcasted_iota(jnp.int32, (8, 128), 1)
    log_grid = (jnp.minimum(lane, 15).astype(F32) * 0.2 - 3.0) * float(np.log(10.0))
    square = jnp.exp(2.0 * log_grid)
    entry_a, entry_b, rest, determ = entries(square)
    inverse = 1.0 / (determ + square * (entry_a + entry_b))
    miss = rest * inverse
    other = b3 + square
    scores = 3.0 * (miss * miss + (b2 * inverse) * ((other * other + a2 * b3) * inverse))
    shifted = scores + 0.05
    shifted = shifted * shifted
    weights = jnp.where(lane < 16, 1.0 / (shifted * shifted), 0.0)
    chosen = jnp.exp(2.0 * (add(weights * log_grid) / add(weights)))
    entry_a, entry_b, rest, determ = entries(chosen)
    c1 = scale / determ
    return c1 * (1.0 + b2 + entry_b), -c1 * scale


def combine_kernel(stat_ref, both_ref, out_ref, rows_ref):
    rows_ref[...] = stat_ref[...].T[0:16]
    c1, c2 = weights_of(rows_ref)

    def rows(n, carry):
        for t in range(24):
            at = pl.ds(pl.multiple_of(n * 192 + t * 8, 8), 8)
            out_ref[at, :] = c1 * both_ref[0, at, :] + c2 * both_ref[1, at, :]
        return carry

    lax.fori_loop(0, 16, rows, 0)


def make_local():
    vmem = pl.BlockSpec(memory_space=pltpu.VMEM)
    smem = pl.BlockSpec(memory_space=pltpu.SMEM)
    hbm = pl.BlockSpec(memory_space=pltpu.HBM)
    params = pltpu.CompilerParams(vmem_limit_bytes=40 << 20)

    depth = halves(depth_basis())
    basis = plane_basis(NX)
    place = np.arange(NX)
    qx = halves(basis[:, 16 * (place // 16) + 4 * (place % 4) + (place // 4) % 4])
    qy = halves(basis.T)
    table = halves(plane_table(NX))
    half_rows = pltpu.VMEM((1536, 128), F32)
    tile = pltpu.VMEM((8, 128), F32)
    planes = pltpu.VMEM((6, NX, NY), F32)

    def exchange(chunks):
        return lax.all_to_all(chunks, ("gx", "gy"), 0, 0, tiled=True)

    def in_hbm(*arrays):
        return [pltpu.with_memory_space_constraint(jnp.asarray(x), pltpu.HBM) for x in arrays]

    def local(observed, psf_taps):
        dev = (lax.axis_index("gx") * 8 + lax.axis_index("gy")).astype(jnp.int32).reshape(1)
        sent = pl.pallas_call(
            forward_z_kernel,
            in_specs=[smem] + [hbm] * 3,
            out_specs=vmem,
            out_shape=pltpu.VMEM((3072, 128), F32),
            scratch_shapes=[pltpu.VMEM((512, NZ), F32)]
            + [pltpu.VMEM((4 * THIRD, THIRD), BF16)] * 2
            + [pltpu.VMEM((2, 4, 256, THIRD), BF16)] * 2
            + [pltpu.SemaphoreType.DMA((4,))],
            compiler_params=params,
            name="forward_z",
        )(dev, *in_hbm(observed.reshape(512, NZ), *depth))
        got = exchange(sent.reshape(128, 24, 128)).reshape(3072, 128)
        spec, stat = pl.pallas_call(
            forward_xy_kernel,
            in_specs=[smem] + [vmem] * 8,
            out_specs=[hbm] * 2,
            out_shape=[pltpu.HBM((6, NX, NY), F32), pltpu.HBM((128, 128), F32)],
            scratch_shapes=[pltpu.VMEM((3, 512, NY), BF16)] * 2
            + [half_rows] * 2
            + [pltpu.VMEM((4, 128, NY), F32), planes, tile, pltpu.VMEM((128, NY), F32), pltpu.VMEM((32, NY), F32)]
            + [pltpu.VMEM((128, 128), F32), pltpu.SemaphoreType.DMA((2,))],
            compiler_params=params,
            name="forward_xy",
        )(dev, got, psf_taps, *table, *qx, *qy)
        stats = exchange(stat.reshape(128, 1, 128)).reshape(128, 128)
        both = pl.pallas_call(
            inverse_xy_kernel,
            in_specs=[smem] + [hbm] * 8,
            out_specs=vmem,
            out_shape=pltpu.VMEM((2, 3072, 128), F32),
            scratch_shapes=[half_rows] * 4
            + [planes, pltpu.VMEM((3, TAPS), F32)]
            + [pltpu.VMEM((32, 2 * NX), BF16)] * 2
            + [pltpu.VMEM((NX, NX), BF16)] * 4
            + [tile, pltpu.VMEM((NX, NY), F32), pltpu.VMEM((24, NY), F32)]
            + [pltpu.SemaphoreType.DMA((8,))],
            compiler_params=params,
            name="inverse_xy",
        )(dev, *in_hbm(spec, psf_taps, *table, *qx, *qy))
        sent = pl.pallas_call(
            combine_kernel,
            in_specs=[vmem] * 2,
            out_specs=vmem,
            out_shape=pltpu.VMEM((3072, 128), F32),
            scratch_shapes=[pltpu.VMEM((16, 128), F32)],
            compiler_params=params,
            name="combine",
        )(stats, both)
        got = exchange(sent.reshape(128, 24, 128)).reshape(3072, 128)
        out = pl.pallas_call(
            inverse_z_kernel,
            in_specs=[vmem] * 3,
            out_specs=hbm,
            out_shape=jax.ShapeDtypeStruct((512, NZ), F32),
            scratch_shapes=[pltpu.VMEM((512, NZ), F32), pltpu.SemaphoreType.DMA((4,))],
            compiler_params=params,
            name="inverse_z",
        )(got, *depth)
        return out.reshape(16, 32, NZ)

    return local


def solution(mesh):
    in_specs = (P("gx", "gy", None), P())
    out_specs = P("gx", "gy", None)
    return jax.shard_map(make_local(), mesh=mesh, in_specs=in_specs, out_specs=out_specs, check_vma=False)
```

```python
import jax
import jax.numpy as jnp
import numpy as np
from jax import lax
from jax.experimental import pallas as pl
from jax.experimental.pallas import tpu as pltpu
from jax.sharding import PartitionSpec as P

NX, NY, NZ, TAPS = 256, 256, 768, 31
HALF = TAPS // 2
THIRD = NZ // 3
ROOT3 = float(np.sqrt(3.0) / 2.0)
F32, BF16 = jnp.float32, jnp.bfloat16
TINY = 1e-30
NN = ((1,), (0,))
NT = ((1,), (1,))


def halves(values):
    hi = np.asarray(values, np.float32).astype(BF16)
    lo = (values - hi.astype(np.float64)).astype(np.float32).astype(BF16)
    return hi, lo


def plane_basis(n):
    pos = np.arange(n)
    freq = np.arange(n // 2)[:, None]
    angle = 2.0 * np.pi * ((freq * pos) % n) / n
    basis = np.concatenate([np.cos(angle), np.sin(angle)]) * np.sqrt(2.0 / n)
    basis[0] = 1.0 / np.sqrt(n)
    basis[n // 2] = np.where(pos % 2 == 0, 1.0, -1.0) / np.sqrt(n)
    return basis


def plane_table(n):
    freq = np.arange(n) % (n // 2)
    freq[n // 2] = n // 2
    turn = ((np.arange(TAPS) - HALF)[:, None] * freq) % n
    table = np.zeros((32, 2 * n))
    table[:TAPS, :n] = np.cos(2.0 * np.pi * turn / n)
    table[:TAPS, n:] = np.where(turn % (n // 2) == 0, 0.0, np.sin(2.0 * np.pi * turn / n))
    return table


def depth_basis():
    pos = np.arange(THIRD)
    dev = np.arange(128)[:, None]

    def blocks(freq):
        angle = 2.0 * np.pi * ((freq * pos) % NZ) / NZ
        return np.sqrt(2.0 / NZ) * np.cos(angle), np.sqrt(2.0 / NZ) * np.sin(angle)

    cos, sin = blocks(3 * dev)
    cos[0] = 1.0 / np.sqrt(NZ)
    sin[0] = np.where(pos % 2 == 0, 1.0, -1.0) / np.sqrt(NZ)
    cos_one, sin_one = blocks(np.concatenate([3 * dev + 1, -(3 * dev + 2)]))
    return np.concatenate([cos, sin, cos_one, sin_one - cos_one, sin_one + cos_one])


def split(values):
    hi = values.astype(BF16)
    return hi, (values - hi.astype(F32)).astype(BF16)


def dot3(left, right, dims=NN):
    def one(a, b):
        return lax.dot_general(a, b, (dims, ((), ())), preferred_element_type=F32)

    return one(left[0], right[0]) + (one(left[0], right[1]) + one(left[1], right[0]))


def lane_total(values):
    return jnp.broadcast_to(jnp.sum(values, axis=1, keepdims=True), (8, 128))


def total(values):
    sums = lane_total(values[:, :128] + values[:, 128:])
    sums = jnp.broadcast_to(jnp.sum(sums, axis=0, keepdims=True), (8, 128))
    return jnp.concatenate([sums, sums], axis=1)


def depth_response(dev, taps):
    row = lax.broadcasted_iota(jnp.int32, (8, 128), 0)
    offset = lax.broadcasted_iota(jnp.int32, (8, 128), 1).astype(F32) - float(HALF)
    pair = dev * 3 + row // 2
    odd = row % 2
    first = pair == 0
    freq = jnp.where(first & (odd == 1), NZ // 2, pair).astype(F32)
    turn = freq * offset
    turn = turn - float(NZ) * jnp.floor(turn * (1.0 / NZ))
    angle = turn * (2.0 * np.pi / NZ)
    real = jnp.sum(jnp.cos(angle) * taps, axis=1, keepdims=True)
    imag = jnp.sum(jnp.where(first, 0.0, jnp.sin(angle)) * taps, axis=1, keepdims=True)
    return real, jnp.where(odd[:, 0:1] == 1, -imag, imag), real * real + imag * imag


def swap_blocks(vecs):
    block = lax.broadcasted_iota(jnp.int32, vecs[0].shape, 1) // 32
    odd, high = (block & 1) != 0, (block & 2) != 0

    def pick(arrays, first):
        pairs = [jnp.where(odd, arrays[(n + 1) % 4], arrays[n]) for n in range(4)]
        return [jnp.where(high, pairs[(n + 2) % 4], pairs[n % 4]) for n in first]

    turned = [pltpu.roll(v, 32 * n, 1) if n else v for n, v in enumerate(pick(vecs, range(4)))]
    return pick(turned, (0, 3, 2, 1))


def plane_response(taps_ref, pad_ref, table):
    pad_ref[...] = jnp.zeros((8, 128), F32)
    pad_ref[0:3, 0:TAPS] = taps_ref[...]
    taps = pad_ref[...]
    rows = dot3(split(taps[:, 0:32]), table)
    cols = rows.T
    lam_x = cols[0:NX, 0:1] * cols[0:NX, 0:1] + cols[NX:, 0:1] * cols[NX:, 0:1]
    lam_y = rows[1:2, 0:NY] * rows[1:2, 0:NY] + rows[1:2, NY:] * rows[1:2, NY:]
    return taps, rows, cols, lam_x, lam_y


def forward_z_kernel(dev_ref, cells_hbm, fh_hbm, fl_hbm, out_ref, cells, fh, fl, half, wide, sems):
    parts = [(cells_hbm, cells, 0, 256), (fh_hbm, fh, 0, 1024), (fl_hbm, fl, 0, 1024), (cells_hbm, cells, 1, 256)]
    copies = []
    for n, (src, dst, block, size) in enumerate(parts):
        rows = pl.ds(block * 256, size)
        copies.append(pltpu.make_async_copy(src.at[rows], dst.at[rows], sems.at[n]))
        copies[n].start()

    def prepare(n):
        for r in range(0, 256, 32):
            b0, b1, b2 = [cells[n * 256 + r : n * 256 + r + 32, m * THIRD : (m + 1) * THIRD] for m in range(3)]
            both = b1 + b2
            p, q = b0 - 0.5 * both, ROOT3 * (b1 - b2)
            for at, value in enumerate((b0 + both, p + q, p, q)):
                half[n, at, r : r + 32, :], wide[n, at, r : r + 32, :] = split(value)

    def store(freqs, p, n):
        for par in range(2):
            for c in range(2):
                out_ref[pl.ds(p * 8 + (2 * n + c) * 2 + par, 128, stride=24), :] = freqs[par][:, c * 128 : (c + 1) * 128]

    def product(block, n):
        rows = slice(block * 256, (block + 1) * 256)
        return dot3((fh[rows, :], fl[rows, :]), (half[n, block], wide[n, block]), NT)


    def transform(n):
        one, two, three = product(1, n), product(2, n), product(3, n)
        real, imag = one - three, one + two
        store((real[0:128], imag[0:128]), 1, n)
        store((real[128:], -imag[128:]), 2, n)
        whole = product(0, n)
        store((whole[0:128], whole[128:]), 0, n)

    copies[0].wait()
    prepare(0)
    copies[1].wait()
    copies[2].wait()
    transform(0)
    copies[3].wait()
    prepare(1)
    transform(1)


def inverse_z_kernel(in_ref, fh_ref, fl_ref, out_hbm, out, sems):
    copies = []

    def product(values, block):
        rows = slice(block * 256, (block + 1) * 256)
        return dot3(split(values), (fh_ref[rows, :], fl_ref[rows, :]))

    for n in range(2):

        def columns(*ks):
            blocks = []
            for c in (2 * n, 2 * n + 1):
                got = [in_ref[pl.ds(k // 2 * 8 + c * 2 + k % 2, 128, stride=24), :].T for k in ks]
                blocks.append(jnp.concatenate(got, axis=1))
            return jnp.concatenate(blocks, axis=0)

        real, imag = columns(2, 4), columns(3, 5)
        imag = jnp.concatenate([imag[:, :128], -imag[:, 128:]], axis=1)
        one, two, three = product(real + imag, 1), product(imag, 2), product(real, 3)
        base = product(columns(0, 1), 0)
        p, q = one + two, ROOT3 * (one - three)
        low = base - 0.5 * p
        for half in range(2):
            rows = slice(half * 128, (half + 1) * 128)
            at = n * 256 + half * 128
            out[at : at + 128, 0:THIRD] = base[rows] + p[rows]
            out[at : at + 128, THIRD : 2 * THIRD] = low[rows] + q[rows]
            out[at : at + 128, 2 * THIRD :] = low[rows] - q[rows]
            here = pl.ds(at, 128)
            copies.append(pltpu.make_async_copy(out.at[here], out_hbm.at[here], sems.at[2 * n + half]))
            copies[-1].start()
    for copy in copies:
        copy.wait()


def forward_xy_kernel(
    dev_ref, in_ref, taps_ref, tabh_ref, tabl_ref, qxh_ref, qxl_ref, qyh_ref, qyl_ref, spec_hbm, stat_hbm, fh_ref, fl_ref,
    lo_ref, hi_ref, weight_ref, spec_ref, pad_ref, lam_ref, zlam_ref, stat_ref, sems,
):
    taps, rows, cols, lam_x, lam_y = plane_response(taps_ref, pad_ref, (tabh_ref[...], tabl_ref[...]))
    lam_ref[...] = lam_x[0:128] * lam_y
    lam_edge = lam_x[128:129] * lam_y
    zlam = jnp.broadcast_to(depth_response(dev_ref[0], taps[2:3, :])[2], (8, NY))
    for slot, k in enumerate((0, 1, 2, 4)):
        zlam_ref[slot * 8 : slot * 8 + 8, :] = jnp.broadcast_to(zlam[k : k + 1, :], (8, NY))
    left, right = (qxh_ref[...], qxl_ref[...]), (qyh_ref[...], qyl_ref[...])

    def gather(p):
        for i in range(16):
            for high in range(2):
                first = [((high * 4 + j) * 16 + i) * 24 + p * 8 for j in range(4)]
                got = swap_blocks([in_ref[at : at + 8, :] for at in first])
                for r in (0, 2):
                    at = slice((i * 4 + r) * 8, (i * 4 + r + 2) * 8)
                    lanes = slice(high * 128, (high + 1) * 128)
                    fh_ref[p, at, lanes], fl_ref[p, at, lanes] = split(jnp.concatenate(got[r : r + 2], axis=0))

    def along_y(p):
        for h in range(2):
            at = slice(h * 256, (h + 1) * 256)
            field = dot3((fh_ref[p, at], fl_ref[p, at]), right)
            at = slice(p * 512 + h * 256, p * 512 + (h + 1) * 256)
            lo_ref[at, :], hi_ref[at, :] = field[:, :128], field[:, 128:]

    top = lax.broadcasted_iota(jnp.int32, (8, NY), 0) == 0
    edges = []
    plain = [jnp.zeros((8, NY), F32)] * 3

    def along_x(p):
        specs = []
        for par in range(2):
            plane = [ref[pl.ds(p * 512 + par, 256, stride=2), :] for ref in (lo_ref, hi_ref)]
            specs.append(dot3(left, split(jnp.concatenate(plane, axis=1))))
        weights = []
        for par, spec in enumerate(specs):
            spec_ref[2 * p + par] = spec
            upper, lower = spec[0:128], spec[128:256]
            upper, lower = upper * upper, lower * lower
            edges.append(lower[0:1, :])
            weights.append(jnp.concatenate([upper[0:8] + jnp.where(top, 0.0, lower[0:8]), upper[8:] + lower[8:]], axis=0))
        for slot, weight in enumerate(weights if p == 0 else [weights[0] + weights[1]], 0 if p == 0 else p + 1):
            weight_ref[slot] = weight
            w = weight.reshape(16, 8, NY)
            l = lam_ref[...].reshape(16, 8, NY) * zlam_ref[slot * 8 : slot * 8 + 8, :]
            for n, value in enumerate((w, w * l, w * l * l)):
                plain[n] = plain[n] + value.sum(axis=0)

    gather(0)
    along_y(0)
    gather(1)
    along_y(1)
    gather(2)
    along_x(0)
    along_y(2)
    along_x(1)
    along_x(2)
    copies = [pltpu.make_async_copy(spec_ref, spec_hbm, sems.at[0])]
    copies[0].start()

    row = lax.broadcasted_iota(jnp.int32, (8, NY), 0)
    edge = jnp.zeros((8, NY), F32)
    for slot, value in enumerate((edges[0], edges[1], edges[2] + edges[3], edges[4] + edges[5])):
        edge = jnp.where(row == slot, value, edge)
    zedge = jnp.where(row < 2, zlam, jnp.where(row == 2, zlam_ref[16:24, :], zlam_ref[24:32, :]))
    edge_lam = lam_edge * zedge

    def sums(*funcs):
        def more(parts, w, l):
            w, l = w.reshape(-1, 8, NY), l.reshape(-1, 8, NY)
            return [part + func(w, l).sum(axis=0) for part, func in zip(parts, funcs)]

        def plane(slot, parts):
            zlam = jnp.concatenate([zlam_ref[pl.ds(pl.multiple_of(slot * 8, 8), 8), :]] * 4, axis=0)
            for r in range(4):
                parts = more(parts, weight_ref[slot, r * 32 : (r + 1) * 32, :], lam_ref[r * 32 : (r + 1) * 32, :] * zlam)
            return parts

        parts = more([jnp.zeros((8, NY), F32) for _ in funcs], edge, edge_lam)
        return [total(p) for p in lax.fori_loop(0, 4, plane, parts)]

    first = edge * edge_lam
    zero, one, two = [total(p) for p in (plain[0] + edge, plain[1] + first, plain[2] + first * edge_lam)]
    mean = one / jnp.maximum(zero, TINY)
    tau = two / jnp.maximum(one, TINY)

    def centred(w, l):
        d = l - mean
        return w * d * d

    def tilted(w, l):
        d = l - tau
        return w * l * d * d

    var, tilt = sums(centred, tilted)
    step = tau - mean
    slope = (tilt + one * step * step) / jnp.maximum(var, TINY)
    ratio = var / jnp.maximum(zero, TINY)

    def second(w, l):
        d = (l - slope) * (l - mean) - ratio
        return w * d * d

    (last,) = sums(second)
    lane = lax.broadcasted_iota(jnp.int32, (8, 128), 1)
    packed = jnp.zeros((8, 128), F32)
    for n, value in enumerate((zero, mean, tau, var, slope, ratio, tilt, last, one)):
        packed = jnp.where(lane == n, value[:, 0:128], packed)
    for n in range(16):
        stat_ref[n * 8 : n * 8 + 8, :] = packed
    copies.append(pltpu.make_async_copy(stat_ref, stat_hbm, sems.at[1]))
    copies[1].start()
    for copy in copies:
        copy.wait()


def inverse_xy_kernel(
    dev_ref, spec_hbm, taps_hbm, tabh_hbm, tabl_hbm, qxh_hbm, qxl_hbm, qyh_hbm, qyl_hbm, out_ref, ulo_ref, uhi_ref, vlo_ref,
    vhi_ref, spec_ref, taps_ref, tabh_ref, tabl_ref, qxh_ref, qxl_ref, qyh_ref, qyl_ref, pad_ref, lam_ref, zed_ref, sems,
):
    pairs = [(taps_hbm, taps_ref), (tabh_hbm, tabh_ref), (tabl_hbm, tabl_ref), (qxh_hbm, qxh_ref), (qxl_hbm, qxl_ref)]
    pairs += [(qyh_hbm, qyh_ref), (qyl_hbm, qyl_ref), (spec_hbm, spec_ref)]
    copies = [pltpu.make_async_copy(src, dst, sems.at[n]) for n, (src, dst) in enumerate(pairs)]
    for copy in copies:
        copy.start()
    for copy in copies[:7]:
        copy.wait()
    taps, rows, cols, lam_x, lam_y = plane_response(taps_ref, pad_ref, (tabh_ref[...], tabl_ref[...]))
    lam_ref[...] = lam_x * lam_y
    for n, value in enumerate(depth_response(dev_ref[0], taps[2:3, :])):
        zed_ref[n * 8 : n * 8 + 8, :] = jnp.broadcast_to(value, (8, NY))
    qt = (qxh_ref[...].astype(F32) + qxl_ref[...].astype(F32)).T
    turned = jnp.concatenate([-qt[:, 128:], qt[:, :128]], axis=1)
    left = split(qt * rows[0:1, 0:NX] + turned * rows[0:1, NX:])
    q = (qyh_ref[...].astype(F32) + qyl_ref[...].astype(F32)).T
    turned = jnp.concatenate([-q[128:, :], q[:128, :]], axis=0)
    right = split(q * cols[0:NY, 1:2] + turned * cols[NY:, 1:2])
    copies[7].wait()
    refs = (ulo_ref, uhi_ref, vlo_ref, vhi_ref)
    for p in range(3):
        e, o = 2 * p, 2 * p + 1
        a, b = spec_ref[e], spec_ref[o]
        lam = lam_ref[...]
        la, lb = a * (lam * zed_ref[16 + e : 17 + e, :]), b * (lam * zed_ref[16 + o : 17 + o, :])
        for k, x, y, lx, ly in ((e, a, b, la, lb), (o, b, a, lb, la)):
            re, im = zed_ref[k : k + 1, :], zed_ref[8 + k : 9 + k, :]
            both = jnp.concatenate([re * x + im * y, re * lx + im * ly], axis=1)
            back = dot3(left, split(both))
            for n, ref in enumerate(refs):
                ref[pl.ds(p * 512 + k % 2, 256, stride=2), :] = back[:, n * 128 : (n + 1) * 128]

        for which, pair in enumerate((refs[0:2], refs[2:4])):
            field = jnp.concatenate([ref[p * 512 : (p + 1) * 512, :] for ref in pair], axis=1)
            field = dot3(split(field), right)
            for i in range(16):
                for high in range(2):
                    got = [field[(i * 4 + r) * 8 : (i * 4 + r + 1) * 8, high * 128 : (high + 1) * 128] for r in range(4)]
                    for j, piece in enumerate(swap_blocks(got)):
                        at = ((high * 4 + j) * 16 + i) * 24 + p * 8
                        out_ref[which, at : at + 8, :] = piece


def weights_of(stats_ref):
    zero, mean, tau, var, slope, ratio, tilt, last, one = [
        jnp.broadcast_to(stats_ref[n : n + 1, :], (8, 128)) for n in range(9)
    ]
    add = lane_total

    all_zero = add(zero)
    all_mean = add(one) / all_zero
    shift = mean - all_mean
    all_var = add(var + shift * shift * zero)
    all_ratio = all_var / all_zero
    lean = tau - all_mean
    all_slope = add(tilt + one * lean * lean) / all_var
    lean = tau - all_mean - all_var / (all_zero * all_mean)
    all_tilt = add(tilt + one * lean * lean)
    first = shift + (slope - all_slope)
    const = shift * (mean - all_slope) + ratio - all_ratio
    all_last = add(last + first * first * var + const * const * zero)

    scale = 1.0 / all_mean
    b2, a2, b3 = all_ratio * (scale * scale), all_tilt / all_var * scale, all_last / all_tilt * scale

    def entries(square):
        entry_a, entry_b = 1.0 + b2 + square, a2 + b3 + square
        rest = b2 * (b3 + square) + square * entry_b
        return entry_a, entry_b, rest, entry_b + rest

    lane = lax.broadcasted_iota(jnp.int32, (8, 128), 1)
    log_grid = (jnp.minimum(lane, 15).astype(F32) * 0.2 - 3.0) * float(np.log(10.0))
    square = jnp.exp(2.0 * log_grid)
    entry_a, entry_b, rest, determ = entries(square)
    inverse = 1.0 / (determ + square * (entry_a + entry_b))
    miss = rest * inverse
    other = b3 + square
    scores = 3.0 * (miss * miss + (b2 * inverse) * ((other * other + a2 * b3) * inverse))
    shifted = scores + 0.05
    shifted = shifted * shifted
    weights = jnp.where(lane < 16, 1.0 / (shifted * shifted), 0.0)
    chosen = jnp.exp(2.0 * (add(weights * log_grid) / add(weights)))
    entry_a, entry_b, rest, determ = entries(chosen)
    c1 = scale / determ
    return c1 * (1.0 + b2 + entry_b), -c1 * scale


def combine_kernel(stat_ref, both_ref, out_ref, rows_ref):
    rows_ref[...] = stat_ref[...].T[0:16]
    c1, c2 = weights_of(rows_ref)

    def rows(n, carry):
        for t in range(24):
            at = pl.ds(pl.multiple_of(n * 192 + t * 8, 8), 8)
            out_ref[at, :] = c1 * both_ref[0, at, :] + c2 * both_ref[1, at, :]
        return carry

    lax.fori_loop(0, 16, rows, 0)


def make_local():
    vmem = pl.BlockSpec(memory_space=pltpu.VMEM)
    smem = pl.BlockSpec(memory_space=pltpu.SMEM)
    hbm = pl.BlockSpec(memory_space=pltpu.HBM)
    params = pltpu.CompilerParams(vmem_limit_bytes=40 << 20)

    depth = halves(depth_basis())
    basis = plane_basis(NX)
    place = np.arange(NX)
    qx = halves(basis[:, 16 * (place // 16) + 4 * (place % 4) + (place // 4) % 4])
    qy = halves(basis.T)
    table = halves(plane_table(NX))
    half_rows = pltpu.VMEM((1536, 128), F32)
    tile = pltpu.VMEM((8, 128), F32)
    planes = pltpu.VMEM((6, NX, NY), F32)

    def exchange(chunks):
        return lax.all_to_all(chunks, ("gy", "gx"), 0, 0, tiled=True)

    def in_hbm(*arrays):
        return [pltpu.with_memory_space_constraint(jnp.asarray(x), pltpu.HBM) for x in arrays]

    def local(observed, psf_taps):
        dev = (lax.axis_index("gy") * 16 + lax.axis_index("gx")).astype(jnp.int32).reshape(1)
        sent = pl.pallas_call(
            forward_z_kernel,
            in_specs=[smem] + [hbm] * 3,
            out_specs=vmem,
            out_shape=pltpu.VMEM((3072, 128), F32),
            scratch_shapes=[pltpu.VMEM((512, NZ), F32)]
            + [pltpu.VMEM((4 * THIRD, THIRD), BF16)] * 2
            + [pltpu.VMEM((2, 4, 256, THIRD), BF16)] * 2
            + [pltpu.SemaphoreType.DMA((4,))],
            compiler_params=params,
            name="forward_z",
        )(dev, *in_hbm(observed.reshape(512, NZ), *depth))
        got = exchange(sent.reshape(128, 24, 128)).reshape(3072, 128)
        spec, stat = pl.pallas_call(
            forward_xy_kernel,
            in_specs=[smem] + [vmem] * 8,
            out_specs=[hbm] * 2,
            out_shape=[pltpu.HBM((6, NX, NY), F32), pltpu.HBM((128, 128), F32)],
            scratch_shapes=[pltpu.VMEM((3, 512, NY), BF16)] * 2
            + [half_rows] * 2
            + [pltpu.VMEM((4, 128, NY), F32), planes, tile, pltpu.VMEM((128, NY), F32), pltpu.VMEM((32, NY), F32)]
            + [pltpu.VMEM((128, 128), F32), pltpu.SemaphoreType.DMA((2,))],
            compiler_params=params,
            name="forward_xy",
        )(dev, got, psf_taps, *table, *qx, *qy)
        stats = exchange(stat.reshape(128, 1, 128)).reshape(128, 128)
        both = pl.pallas_call(
            inverse_xy_kernel,
            in_specs=[smem] + [hbm] * 8,
            out_specs=vmem,
            out_shape=pltpu.VMEM((2, 3072, 128), F32),
            scratch_shapes=[half_rows] * 4
            + [planes, pltpu.VMEM((3, TAPS), F32)]
            + [pltpu.VMEM((32, 2 * NX), BF16)] * 2
            + [pltpu.VMEM((NX, NX), BF16)] * 4
            + [tile, pltpu.VMEM((NX, NY), F32), pltpu.VMEM((24, NY), F32)]
            + [pltpu.SemaphoreType.DMA((8,))],
            compiler_params=params,
            name="inverse_xy",
        )(dev, *in_hbm(spec, psf_taps, *table, *qx, *qy))
        sent = pl.pallas_call(
            combine_kernel,
            in_specs=[vmem] * 2,
            out_specs=vmem,
            out_shape=pltpu.VMEM((3072, 128), F32),
            scratch_shapes=[pltpu.VMEM((16, 128), F32)],
            compiler_params=params,
            name="combine",
        )(stats, both)
        got = exchange(sent.reshape(128, 24, 128)).reshape(3072, 128)
        out = pl.pallas_call(
            inverse_z_kernel,
            in_specs=[vmem] * 3,
            out_specs=hbm,
            out_shape=jax.ShapeDtypeStruct((512, NZ), F32),
            scratch_shapes=[pltpu.VMEM((512, NZ), F32), pltpu.SemaphoreType.DMA((4,))],
            compiler_params=params,
            name="inverse_z",
        )(got, *depth)
        return out.reshape(16, 32, NZ)

    return local


def solution(mesh):
    in_specs = (P("gx", "gy", None), P())
    out_specs = P("gx", "gy", None)
    return jax.shard_map(make_local(), mesh=mesh, in_specs=in_specs, out_specs=out_specs, check_vma=False)
```

```python
import jax
import jax.numpy as jnp
import numpy as np
from jax import lax
from jax.experimental import pallas as pl
from jax.experimental.pallas import tpu as pltpu
from jax.sharding import PartitionSpec as P

NX, NY, NZ, TAPS = 256, 256, 768, 31
HALF = TAPS // 2
THIRD = NZ // 3
ROOT3 = float(np.sqrt(3.0) / 2.0)
F32, BF16 = jnp.float32, jnp.bfloat16
TINY = 1e-30
NN = ((1,), (0,))
NT = ((1,), (1,))


def halves(values):
    hi = np.asarray(values, np.float32).astype(BF16)
    lo = (values - hi.astype(np.float64)).astype(np.float32).astype(BF16)
    return hi, lo


def plane_basis(n):
    pos = np.arange(n)
    freq = np.arange(n // 2)[:, None]
    angle = 2.0 * np.pi * ((freq * pos) % n) / n
    basis = np.concatenate([np.cos(angle), np.sin(angle)]) * np.sqrt(2.0 / n)
    basis[0] = 1.0 / np.sqrt(n)
    basis[n // 2] = np.where(pos % 2 == 0, 1.0, -1.0) / np.sqrt(n)
    return basis


def plane_table(n):
    freq = np.arange(n) % (n // 2)
    freq[n // 2] = n // 2
    turn = ((np.arange(TAPS) - HALF)[:, None] * freq) % n
    table = np.zeros((32, 2 * n))
    table[:TAPS, :n] = np.cos(2.0 * np.pi * turn / n)
    table[:TAPS, n:] = np.where(turn % (n // 2) == 0, 0.0, np.sin(2.0 * np.pi * turn / n))
    return table


def depth_basis():
    pos = np.arange(THIRD)
    dev = np.arange(128)[:, None]

    def blocks(freq):
        angle = 2.0 * np.pi * ((freq * pos) % NZ) / NZ
        return np.sqrt(2.0 / NZ) * np.cos(angle), np.sqrt(2.0 / NZ) * np.sin(angle)

    cos, sin = blocks(3 * dev)
    cos[0] = 1.0 / np.sqrt(NZ)
    sin[0] = np.where(pos % 2 == 0, 1.0, -1.0) / np.sqrt(NZ)
    cos_one, sin_one = blocks(np.concatenate([3 * dev + 1, -(3 * dev + 2)]))
    return np.concatenate([cos, sin, cos_one, sin_one - cos_one, sin_one + cos_one])


def split(values):
    hi = values.astype(BF16)
    return hi, (values - hi.astype(F32)).astype(BF16)


def dot3(left, right, dims=NN):
    def one(a, b):
        return lax.dot_general(a, b, (dims, ((), ())), preferred_element_type=F32)

    return one(left[0], right[0]) + (one(left[0], right[1]) + one(left[1], right[0]))


def lane_total(values):
    return jnp.broadcast_to(jnp.sum(values, axis=1, keepdims=True), (8, 128))


def total(values):
    sums = lane_total(values[:, :128] + values[:, 128:])
    sums = jnp.broadcast_to(jnp.sum(sums, axis=0, keepdims=True), (8, 128))
    return jnp.concatenate([sums, sums], axis=1)


def depth_response(dev, taps):
    row = lax.broadcasted_iota(jnp.int32, (8, 128), 0)
    offset = lax.broadcasted_iota(jnp.int32, (8, 128), 1).astype(F32) - float(HALF)
    pair = dev * 3 + row // 2
    odd = row % 2
    first = pair == 0
    freq = jnp.where(first & (odd == 1), NZ // 2, pair).astype(F32)
    turn = freq * offset
    turn = turn - float(NZ) * jnp.floor(turn * (1.0 / NZ))
    angle = turn * (2.0 * np.pi / NZ)
    real = jnp.sum(jnp.cos(angle) * taps, axis=1, keepdims=True)
    imag = jnp.sum(jnp.where(first, 0.0, jnp.sin(angle)) * taps, axis=1, keepdims=True)
    return real, jnp.where(odd[:, 0:1] == 1, -imag, imag), real * real + imag * imag


def swap_blocks(vecs):
    block = lax.broadcasted_iota(jnp.int32, vecs[0].shape, 1) // 32
    odd, high = (block & 1) != 0, (block & 2) != 0

    def pick(arrays, first):
        pairs = [jnp.where(odd, arrays[(n + 1) % 4], arrays[n]) for n in range(4)]
        return [jnp.where(high, pairs[(n + 2) % 4], pairs[n % 4]) for n in first]

    turned = [pltpu.roll(v, 32 * n, 1) if n else v for n, v in enumerate(pick(vecs, range(4)))]
    return pick(turned, (0, 3, 2, 1))


def plane_response(taps_ref, pad_ref, table):
    pad_ref[...] = jnp.zeros((8, 128), F32)
    pad_ref[0:3, 0:TAPS] = taps_ref[...]
    taps = pad_ref[...]
    rows = dot3(split(taps[:, 0:32]), table)
    cols = rows.T
    lam_x = cols[0:NX, 0:1] * cols[0:NX, 0:1] + cols[NX:, 0:1] * cols[NX:, 0:1]
    lam_y = rows[1:2, 0:NY] * rows[1:2, 0:NY] + rows[1:2, NY:] * rows[1:2, NY:]
    return taps, rows, cols, lam_x, lam_y


def forward_z_kernel(dev_ref, cells_hbm, fh_hbm, fl_hbm, out_ref, cells, fh, fl, half, wide, sems):
    parts = [(cells_hbm, cells, 0, 256), (fh_hbm, fh, 0, 1024), (fl_hbm, fl, 0, 1024), (cells_hbm, cells, 1, 256)]
    copies = []
    for n, (src, dst, block, size) in enumerate(parts):
        rows = pl.ds(block * 256, size)
        copies.append(pltpu.make_async_copy(src.at[rows], dst.at[rows], sems.at[n]))
        copies[n].start()

    def prepare(n):
        for r in range(0, 256, 32):
            b0, b1, b2 = [cells[n * 256 + r : n * 256 + r + 32, m * THIRD : (m + 1) * THIRD] for m in range(3)]
            both = b1 + b2
            p, q = b0 - 0.5 * both, ROOT3 * (b1 - b2)
            for at, value in enumerate((b0 + both, p + q, p, q)):
                half[n, at, r : r + 32, :], wide[n, at, r : r + 32, :] = split(value)

    def store(freqs, p, n):
        for par in range(2):
            for c in range(2):
                out_ref[pl.ds(p * 8 + (2 * n + c) * 2 + par, 128, stride=24), :] = freqs[par][:, c * 128 : (c + 1) * 128]

    def product(block, n):
        rows = slice(block * 256, (block + 1) * 256)
        return dot3((fh[rows, :], fl[rows, :]), (half[n, block], wide[n, block]), NT)


    def transform(n):
        one, two, three = product(1, n), product(2, n), product(3, n)
        real, imag = one - three, one + two
        store((real[0:128], imag[0:128]), 1, n)
        store((real[128:], -imag[128:]), 2, n)
        whole = product(0, n)
        store((whole[0:128], whole[128:]), 0, n)

    copies[0].wait()
    prepare(0)
    copies[1].wait()
    copies[2].wait()
    transform(0)
    copies[3].wait()
    prepare(1)
    transform(1)


def inverse_z_kernel(in_ref, fh_ref, fl_ref, out_hbm, out, sems):
    copies = []

    def product(values, block):
        rows = slice(block * 256, (block + 1) * 256)
        return dot3(split(values), (fh_ref[rows, :], fl_ref[rows, :]))

    for n in range(2):

        def columns(*ks):
            blocks = []
            for c in (2 * n, 2 * n + 1):
                got = [in_ref[pl.ds(k // 2 * 8 + c * 2 + k % 2, 128, stride=24), :].T for k in ks]
                blocks.append(jnp.concatenate(got, axis=1))
            return jnp.concatenate(blocks, axis=0)

        real, imag = columns(2, 4), columns(3, 5)
        imag = jnp.concatenate([imag[:, :128], -imag[:, 128:]], axis=1)
        one, two, three = product(real + imag, 1), product(imag, 2), product(real, 3)
        base = product(columns(0, 1), 0)
        p, q = one + two, ROOT3 * (one - three)
        low = base - 0.5 * p
        for half in range(2):
            rows = slice(half * 128, (half + 1) * 128)
            at = n * 256 + half * 128
            out[at : at + 128, 0:THIRD] = base[rows] + p[rows]
            out[at : at + 128, THIRD : 2 * THIRD] = low[rows] + q[rows]
            out[at : at + 128, 2 * THIRD :] = low[rows] - q[rows]
            here = pl.ds(at, 128)
            copies.append(pltpu.make_async_copy(out.at[here], out_hbm.at[here], sems.at[2 * n + half]))
            copies[-1].start()
    for copy in copies:
        copy.wait()


def forward_xy_kernel(
    dev_ref, in_ref, taps_ref, tabh_ref, tabl_ref, qxh_ref, qxl_ref, qyh_ref, qyl_ref, spec_hbm, stat_hbm, fh_ref, fl_ref,
    lo_ref, hi_ref, weight_ref, spec_ref, pad_ref, lam_ref, zlam_ref, stat_ref, sems,
):
    taps, rows, cols, lam_x, lam_y = plane_response(taps_ref, pad_ref, (tabh_ref[...], tabl_ref[...]))
    lam_ref[...] = lam_x[0:128] * lam_y
    lam_edge = lam_x[128:129] * lam_y
    zlam = jnp.broadcast_to(depth_response(dev_ref[0], taps[2:3, :])[2], (8, NY))
    for slot, k in enumerate((0, 1, 2, 4)):
        zlam_ref[slot * 8 : slot * 8 + 8, :] = jnp.broadcast_to(zlam[k : k + 1, :], (8, NY))
    left, right = (qxh_ref[...], qxl_ref[...]), (qyh_ref[...], qyl_ref[...])

    def gather(p):
        for i in range(16):
            for high in range(2):
                first = [((high * 4 + j) * 16 + i) * 24 + p * 8 for j in range(4)]
                got = swap_blocks([in_ref[at : at + 8, :] for at in first])
                for r in (0, 2):
                    at = slice((i * 4 + r) * 8, (i * 4 + r + 2) * 8)
                    lanes = slice(high * 128, (high + 1) * 128)
                    fh_ref[p, at, lanes], fl_ref[p, at, lanes] = split(jnp.concatenate(got[r : r + 2], axis=0))

    def along_y(p):
        for h in range(2):
            at = slice(h * 256, (h + 1) * 256)
            field = dot3((fh_ref[p, at], fl_ref[p, at]), right)
            at = slice(p * 512 + h * 256, p * 512 + (h + 1) * 256)
            lo_ref[at, :], hi_ref[at, :] = field[:, :128], field[:, 128:]

    top = lax.broadcasted_iota(jnp.int32, (8, NY), 0) == 0
    edges = []
    plain = [jnp.zeros((8, NY), F32)] * 3

    def along_x(p):
        specs = []
        for par in range(2):
            plane = [ref[pl.ds(p * 512 + par, 256, stride=2), :] for ref in (lo_ref, hi_ref)]
            specs.append(dot3(left, split(jnp.concatenate(plane, axis=1))))
        weights = []
        for par, spec in enumerate(specs):
            spec_ref[2 * p + par] = spec
            upper, lower = spec[0:128], spec[128:256]
            upper, lower = upper * upper, lower * lower
            edges.append(lower[0:1, :])
            weights.append(jnp.concatenate([upper[0:8] + jnp.where(top, 0.0, lower[0:8]), upper[8:] + lower[8:]], axis=0))
        for slot, weight in enumerate(weights if p == 0 else [weights[0] + weights[1]], 0 if p == 0 else p + 1):
            weight_ref[slot] = weight
            w = weight.reshape(16, 8, NY)
            l = lam_ref[...].reshape(16, 8, NY) * zlam_ref[slot * 8 : slot * 8 + 8, :]
            for n, value in enumerate((w, w * l, w * l * l)):
                plain[n] = plain[n] + value.sum(axis=0)

    gather(0)
    gather(1)
    along_y(0)
    along_y(1)
    gather(2)
    along_x(0)
    along_y(2)
    along_x(1)
    along_x(2)
    copies = [pltpu.make_async_copy(spec_ref, spec_hbm, sems.at[0])]
    copies[0].start()

    row = lax.broadcasted_iota(jnp.int32, (8, NY), 0)
    edge = jnp.zeros((8, NY), F32)
    for slot, value in enumerate((edges[0], edges[1], edges[2] + edges[3], edges[4] + edges[5])):
        edge = jnp.where(row == slot, value, edge)
    zedge = jnp.where(row < 2, zlam, jnp.where(row == 2, zlam_ref[16:24, :], zlam_ref[24:32, :]))
    edge_lam = lam_edge * zedge

    def sums(*funcs):
        def more(parts, w, l):
            w, l = w.reshape(-1, 8, NY), l.reshape(-1, 8, NY)
            return [part + func(w, l).sum(axis=0) for part, func in zip(parts, funcs)]

        def plane(slot, parts):
            zlam = jnp.concatenate([zlam_ref[pl.ds(pl.multiple_of(slot * 8, 8), 8), :]] * 4, axis=0)
            for r in range(4):
                parts = more(parts, weight_ref[slot, r * 32 : (r + 1) * 32, :], lam_ref[r * 32 : (r + 1) * 32, :] * zlam)
            return parts

        parts = more([jnp.zeros((8, NY), F32) for _ in funcs], edge, edge_lam)
        return [total(p) for p in lax.fori_loop(0, 4, plane, parts, unroll=4)]

    first = edge * edge_lam
    zero, one, two = [total(p) for p in (plain[0] + edge, plain[1] + first, plain[2] + first * edge_lam)]
    mean = one / jnp.maximum(zero, TINY)
    tau = two / jnp.maximum(one, TINY)

    def centred(w, l):
        d = l - mean
        return w * d * d

    def tilted(w, l):
        d = l - tau
        return w * l * d * d

    var, tilt = sums(centred, tilted)
    step = tau - mean
    slope = (tilt + one * step * step) / jnp.maximum(var, TINY)
    ratio = var / jnp.maximum(zero, TINY)

    def second(w, l):
        d = (l - slope) * (l - mean) - ratio
        return w * d * d

    (last,) = sums(second)
    lane = lax.broadcasted_iota(jnp.int32, (8, 128), 1)
    packed = jnp.zeros((8, 128), F32)
    for n, value in enumerate((zero, mean, tau, var, slope, ratio, tilt, last, one)):
        packed = jnp.where(lane == n, value[:, 0:128], packed)
    for n in range(16):
        stat_ref[n * 8 : n * 8 + 8, :] = packed
    copies.append(pltpu.make_async_copy(stat_ref, stat_hbm, sems.at[1]))
    copies[1].start()
    for copy in copies:
        copy.wait()


def inverse_xy_kernel(
    dev_ref, spec_hbm, taps_hbm, tabh_hbm, tabl_hbm, qxh_hbm, qxl_hbm, qyh_hbm, qyl_hbm, out_ref, ulo_ref, uhi_ref, vlo_ref,
    vhi_ref, spec_ref, taps_ref, tabh_ref, tabl_ref, qxh_ref, qxl_ref, qyh_ref, qyl_ref, pad_ref, lam_ref, zed_ref, sems,
):
    pairs = [(taps_hbm, taps_ref), (tabh_hbm, tabh_ref), (tabl_hbm, tabl_ref), (qxh_hbm, qxh_ref), (qxl_hbm, qxl_ref)]
    pairs += [(qyh_hbm, qyh_ref), (qyl_hbm, qyl_ref), (spec_hbm, spec_ref)]
    copies = [pltpu.make_async_copy(src, dst, sems.at[n]) for n, (src, dst) in enumerate(pairs)]
    for copy in copies:
        copy.start()
    for copy in copies[:7]:
        copy.wait()
    taps, rows, cols, lam_x, lam_y = plane_response(taps_ref, pad_ref, (tabh_ref[...], tabl_ref[...]))
    lam_ref[...] = lam_x * lam_y
    for n, value in enumerate(depth_response(dev_ref[0], taps[2:3, :])):
        zed_ref[n * 8 : n * 8 + 8, :] = jnp.broadcast_to(value, (8, NY))
    qt = (qxh_ref[...].astype(F32) + qxl_ref[...].astype(F32)).T
    turned = jnp.concatenate([-qt[:, 128:], qt[:, :128]], axis=1)
    left = split(qt * rows[0:1, 0:NX] + turned * rows[0:1, NX:])
    q = (qyh_ref[...].astype(F32) + qyl_ref[...].astype(F32)).T
    turned = jnp.concatenate([-q[128:, :], q[:128, :]], axis=0)
    right = split(q * cols[0:NY, 1:2] + turned * cols[NY:, 1:2])
    copies[7].wait()
    refs = (ulo_ref, uhi_ref, vlo_ref, vhi_ref)
    for p in range(3):
        e, o = 2 * p, 2 * p + 1
        a, b = spec_ref[e], spec_ref[o]
        lam = lam_ref[...]
        la, lb = a * (lam * zed_ref[16 + e : 17 + e, :]), b * (lam * zed_ref[16 + o : 17 + o, :])
        for k, x, y, lx, ly in ((e, a, b, la, lb), (o, b, a, lb, la)):
            re, im = zed_ref[k : k + 1, :], zed_ref[8 + k : 9 + k, :]
            both = jnp.concatenate([re * x + im * y, re * lx + im * ly], axis=1)
            back = dot3(left, split(both))
            for n, ref in enumerate(refs):
                ref[pl.ds(p * 512 + k % 2, 256, stride=2), :] = back[:, n * 128 : (n + 1) * 128]

        for which, pair in enumerate((refs[0:2], refs[2:4])):
            field = jnp.concatenate([ref[p * 512 : (p + 1) * 512, :] for ref in pair], axis=1)
            field = dot3(split(field), right)
            for i in range(16):
                for high in range(2):
                    got = [field[(i * 4 + r) * 8 : (i * 4 + r + 1) * 8, high * 128 : (high + 1) * 128] for r in range(4)]
                    for j, piece in enumerate(swap_blocks(got)):
                        at = ((high * 4 + j) * 16 + i) * 24 + p * 8
                        out_ref[which, at : at + 8, :] = piece


def weights_of(stats_ref):
    zero, mean, tau, var, slope, ratio, tilt, last, one = [
        jnp.broadcast_to(stats_ref[n : n + 1, :], (8, 128)) for n in range(9)
    ]
    add = lane_total

    all_zero = add(zero)
    all_mean = add(one) / all_zero
    shift = mean - all_mean
    all_var = add(var + shift * shift * zero)
    all_ratio = all_var / all_zero
    lean = tau - all_mean
    all_slope = add(tilt + one * lean * lean) / all_var
    lean = tau - all_mean - all_var / (all_zero * all_mean)
    all_tilt = add(tilt + one * lean * lean)
    first = shift + (slope - all_slope)
    const = shift * (mean - all_slope) + ratio - all_ratio
    all_last = add(last + first * first * var + const * const * zero)

    scale = 1.0 / all_mean
    b2, a2, b3 = all_ratio * (scale * scale), all_tilt / all_var * scale, all_last / all_tilt * scale

    def entries(square):
        entry_a, entry_b = 1.0 + b2 + square, a2 + b3 + square
        rest = b2 * (b3 + square) + square * entry_b
        return entry_a, entry_b, rest, entry_b + rest

    lane = lax.broadcasted_iota(jnp.int32, (8, 128), 1)
    log_grid = (jnp.minimum(lane, 15).astype(F32) * 0.2 - 3.0) * float(np.log(10.0))
    square = jnp.exp(2.0 * log_grid)
    entry_a, entry_b, rest, determ = entries(square)
    inverse = 1.0 / (determ + square * (entry_a + entry_b))
    miss = rest * inverse
    other = b3 + square
    scores = 3.0 * (miss * miss + (b2 * inverse) * ((other * other + a2 * b3) * inverse))
    shifted = scores + 0.05
    shifted = shifted * shifted
    weights = jnp.where(lane < 16, 1.0 / (shifted * shifted), 0.0)
    chosen = jnp.exp(2.0 * (add(weights * log_grid) / add(weights)))
    entry_a, entry_b, rest, determ = entries(chosen)
    c1 = scale / determ
    return c1 * (1.0 + b2 + entry_b), -c1 * scale


def combine_kernel(stat_ref, both_ref, out_ref, rows_ref):
    rows_ref[...] = stat_ref[...].T[0:16]
    c1, c2 = weights_of(rows_ref)

    def rows(n, carry):
        for t in range(24):
            at = pl.ds(pl.multiple_of(n * 192 + t * 8, 8), 8)
            out_ref[at, :] = c1 * both_ref[0, at, :] + c2 * both_ref[1, at, :]
        return carry

    lax.fori_loop(0, 16, rows, 0)


def make_local():
    vmem = pl.BlockSpec(memory_space=pltpu.VMEM)
    smem = pl.BlockSpec(memory_space=pltpu.SMEM)
    hbm = pl.BlockSpec(memory_space=pltpu.HBM)
    params = pltpu.CompilerParams(vmem_limit_bytes=40 << 20)

    depth = halves(depth_basis())
    basis = plane_basis(NX)
    place = np.arange(NX)
    qx = halves(basis[:, 16 * (place // 16) + 4 * (place % 4) + (place // 4) % 4])
    qy = halves(basis.T)
    table = halves(plane_table(NX))
    half_rows = pltpu.VMEM((1536, 128), F32)
    tile = pltpu.VMEM((8, 128), F32)
    planes = pltpu.VMEM((6, NX, NY), F32)

    def exchange(chunks):
        return lax.all_to_all(chunks, ("gy", "gx"), 0, 0, tiled=True)

    def in_hbm(*arrays):
        return [pltpu.with_memory_space_constraint(jnp.asarray(x), pltpu.HBM) for x in arrays]

    def local(observed, psf_taps):
        dev = (lax.axis_index("gy") * 16 + lax.axis_index("gx")).astype(jnp.int32).reshape(1)
        sent = pl.pallas_call(
            forward_z_kernel,
            in_specs=[smem] + [hbm] * 3,
            out_specs=vmem,
            out_shape=pltpu.VMEM((3072, 128), F32),
            scratch_shapes=[pltpu.VMEM((512, NZ), F32)]
            + [pltpu.VMEM((4 * THIRD, THIRD), BF16)] * 2
            + [pltpu.VMEM((2, 4, 256, THIRD), BF16)] * 2
            + [pltpu.SemaphoreType.DMA((4,))],
            compiler_params=params,
            name="forward_z",
        )(dev, *in_hbm(observed.reshape(512, NZ), *depth))
        got = exchange(sent.reshape(128, 24, 128)).reshape(3072, 128)
        spec, stat = pl.pallas_call(
            forward_xy_kernel,
            in_specs=[smem] + [vmem] * 8,
            out_specs=[hbm] * 2,
            out_shape=[pltpu.HBM((6, NX, NY), F32), pltpu.HBM((128, 128), F32)],
            scratch_shapes=[pltpu.VMEM((3, 512, NY), BF16)] * 2
            + [half_rows] * 2
            + [pltpu.VMEM((4, 128, NY), F32), planes, tile, pltpu.VMEM((128, NY), F32), pltpu.VMEM((32, NY), F32)]
            + [pltpu.VMEM((128, 128), F32), pltpu.SemaphoreType.DMA((2,))],
            compiler_params=params,
            name="forward_xy",
        )(dev, got, psf_taps, *table, *qx, *qy)
        stats = exchange(stat.reshape(128, 1, 128)).reshape(128, 128)
        both = pl.pallas_call(
            inverse_xy_kernel,
            in_specs=[smem] + [hbm] * 8,
            out_specs=vmem,
            out_shape=pltpu.VMEM((2, 3072, 128), F32),
            scratch_shapes=[half_rows] * 4
            + [planes, pltpu.VMEM((3, TAPS), F32)]
            + [pltpu.VMEM((32, 2 * NX), BF16)] * 2
            + [pltpu.VMEM((NX, NX), BF16)] * 4
            + [tile, pltpu.VMEM((NX, NY), F32), pltpu.VMEM((24, NY), F32)]
            + [pltpu.SemaphoreType.DMA((8,))],
            compiler_params=params,
            name="inverse_xy",
        )(dev, *in_hbm(spec, psf_taps, *table, *qx, *qy))
        sent = pl.pallas_call(
            combine_kernel,
            in_specs=[vmem] * 2,
            out_specs=vmem,
            out_shape=pltpu.VMEM((3072, 128), F32),
            scratch_shapes=[pltpu.VMEM((16, 128), F32)],
            compiler_params=params,
            name="combine",
        )(stats, both)
        got = exchange(sent.reshape(128, 24, 128)).reshape(3072, 128)
        out = pl.pallas_call(
            inverse_z_kernel,
            in_specs=[vmem] * 3,
            out_specs=hbm,
            out_shape=jax.ShapeDtypeStruct((512, NZ), F32),
            scratch_shapes=[pltpu.VMEM((512, NZ), F32), pltpu.SemaphoreType.DMA((4,))],
            compiler_params=params,
            name="inverse_z",
        )(got, *depth)
        return out.reshape(16, 32, NZ)

    return local


def solution(mesh):
    in_specs = (P("gx", "gy", None), P())
    out_specs = P("gx", "gy", None)
    return jax.shard_map(make_local(), mesh=mesh, in_specs=in_specs, out_specs=out_specs, check_vma=False)
```
